32 devices in a mesh: blk: 4 (over x, core), uly: 8 (over z, y).
Axes of the slice: x: 2, y: 2, z: 4, core: 2. Of those that a mesh axis runs over, the one named last changes fastest.
Arguments:
- query_rows: bfloat16 [4096, 512], P(('blk', 'uly')), may hold values from -6 to 6
- key_rows: bfloat16 [4096, 512], P(('blk', 'uly')), may hold values from -6 to 6
- value_rows: bfloat16 [4096, 512], P(('blk', 'uly')), may hold values from -6 to 6
- out_grad: bfloat16 [4096, 512], P(('blk', 'uly')), may hold values from -6 to 6
- block_lists: int32 [64, 8], P('blk'), may hold values from 0 to 63, as said below
- block_counts: int32 [64], P('blk'), may hold values from 1 to 8
Outputs:
- attended: bfloat16 [4096, 512], P(('blk', 'uly'))
- query_gradient: bfloat16 [4096, 512], P(('blk', 'uly'))
- key_grad: bfloat16 [4096, 512], P(('blk', 'uly'))
- value_grad: bfloat16 [4096, 512], P(('blk', 'uly'))
The draws below stay inside these ranges and needn't reach their ends.
Inputs may be any that keep to these rules, and one draw needn't show every extreme that they name: `block_lists`: row b lists key blocks of query block b: entry 0 is b, entries 1 to block_counts[b] - 1 are distinct blocks other than b, and the remaining entries equal b.
All inputs are finite; a program needn't handle non-finite values.
Results may differ from the reference program's by a relative error of at most 0.02.
Values may be sent and summed in bfloat16 or wider, within the bound.
A program may use at most 128 MiB of HBM per device.

```python
import math
import jax
import jax.numpy as jnp
from jax import lax

HDIM = 64
BLK = 64
KSEL = 8
HEADS = 8
WIDTH = 512
TOKENS = 4096
NQB = 64


def routing_pair(key):
    base = jax.random.fold_in(key, 11)
    count_key, list_key = jax.random.split(base)
    counts = jax.random.randint(count_key, (NQB,), 1, KSEL + 1)
    counts = counts.at[0].set(KSEL).at[1].set(1)
    own = jnp.arange(NQB)
    logit_matrix = jax.random.randint(list_key, (NQB, NQB), 0, 4096) * NQB + own[None, :]
    logit_matrix = jnp.where(own[:, None] == own[None, :], 4096 * NQB + NQB, logit_matrix)
    chosen = lax.top_k(logit_matrix, KSEL)[1]
    slot_ids = jnp.arange(KSEL)[None, :]
    lists = jnp.where(slot_ids < counts[:, None], chosen, own[:, None])
    return (lists.astype(jnp.int32), counts.astype(jnp.int32))


def draw_block_lists(key, part):
    return routing_pair(key)[0]


def draw_block_counts(key, part):
    return routing_pair(key)[1]


def query_key_pair(key):
    base = jax.random.fold_in(key, 23)
    query_key, key_key = jax.random.split(base, 2)
    shape = (TOKENS, HEADS, HDIM)
    query_matrix = jnp.clip(jax.random.normal(query_key, shape, jnp.float32), -6.0, 6.0)
    keys_drawn = jnp.clip(jax.random.normal(key_key, shape, jnp.float32), -6.0, 6.0)
    return (query_matrix.reshape(TOKENS, WIDTH), keys_drawn.reshape(TOKENS, WIDTH))


def draw_query_rows(key, part):
    return query_key_pair(key)[0].astype(jnp.bfloat16)


def draw_key_rows(key, part):
    return query_key_pair(key)[1].astype(jnp.bfloat16)


def steps_of(rng, shape, cuts, low, largest):
    def one(dim, shards_of):
        heights = jax.random.uniform(jax.random.fold_in(jax.random.fold_in(rng, 6), dim), (shards_of,), jnp.float32, low / len(cuts), largest / len(cuts))
        return jnp.repeat(jnp.exp(heights), shape[dim] // shards_of).reshape((-1,) + (1,) * (len(shape) - dim - 1))

    loudness = one(*cuts[0])
    for cut in cuts[1:]:
        loudness = loudness * one(*cut)
    return loudness


def gaussian(key, shape, deviation, bound, shards=(), kind=jnp.bfloat16):
    loudness = steps_of(key, shape, shards, -0.22, 0.18) if shards else 1.0
    result = jax.random.normal(key, shape, jnp.float32) * deviation * loudness
    return jnp.minimum(jnp.maximum(result, -bound), bound).astype(kind)


def setup_inputs(seed: int = 0) -> dict:
    key_of = jax.random.split(jax.random.key(seed), 7)
    return {
        "query_rows": draw_query_rows(jax.random.fold_in(key_of[6], 71), 0),
        "key_rows": draw_key_rows(jax.random.fold_in(key_of[6], 71), 0),
        "value_rows": gaussian(key_of[2], (TOKENS, WIDTH), 1.0, 6.0, ((0, 32),)),
        "out_grad": gaussian(key_of[3], (TOKENS, WIDTH), 1.0, 6.0, ((0, 32),)),
        "block_lists": draw_block_lists(jax.random.fold_in(key_of[6], 71), 0),
        "block_counts": draw_block_counts(jax.random.fold_in(key_of[6], 71), 0),
    }


def head_pass(operands, block_lists, block_counts):
    query_head, key_head, value_head, grad_head = operands
    softmax_scale = 1.0 / math.sqrt(HDIM)
    query_matrix = query_head.reshape(NQB, BLK, HDIM).astype(jnp.float32)
    gradient_tuple = grad_head.reshape(NQB, BLK, HDIM).astype(jnp.float32)
    gathered_key_blocks = key_head.reshape(NQB, BLK, HDIM)[block_lists].astype(jnp.float32)
    gathered_value_blocks = value_head.reshape(NQB, BLK, HDIM)[block_lists].astype(jnp.float32)
    usable = (jnp.arange(KSEL)[None, :] < block_counts[:, None])[:, None, :, None]
    logit_matrix = jnp.einsum('yxe,yale->yxal', query_matrix, gathered_key_blocks) * softmax_scale
    row_max = lax.optimization_barrier(jnp.max(jnp.where(usable, logit_matrix, -1e+30), axis=(2, 3), keepdims=True))
    weights = jnp.where(usable, jnp.exp(logit_matrix - row_max), 0.0)
    probability = weights / lax.optimization_barrier(jnp.sum(weights, axis=(2, 3), keepdims=True))
    reduced_precision = lax.optimization_barrier(probability.astype(jnp.bfloat16)).astype(jnp.float32)
    attended = jnp.einsum('mexl,mxlf->mef', reduced_precision, gathered_value_blocks).astype(jnp.bfloat16)
    delta = lax.optimization_barrier(jnp.sum(gradient_tuple * attended.astype(jnp.float32), axis=-1))[:, :, None, None]
    probability_gradient = jnp.einsum('yxe,yale->yxal', gradient_tuple, gathered_value_blocks)
    score_gradient = lax.optimization_barrier((probability * (probability_gradient - delta)).astype(jnp.bfloat16)).astype(jnp.float32)
    query_gradient = (jnp.einsum('mexl,mxlf->mef', score_gradient, gathered_key_blocks) * softmax_scale).astype(jnp.bfloat16)
    key_contribution = jnp.einsum('nmpc,nmu->npcu', score_gradient, query_matrix) * softmax_scale
    value_contribution = jnp.einsum('nmpc,nmu->npcu', reduced_precision, gradient_tuple)
    key_grad = jnp.zeros((NQB, BLK, HDIM), jnp.float32).at[block_lists].add(key_contribution).astype(jnp.bfloat16)
    value_grad = jnp.zeros((NQB, BLK, HDIM), jnp.float32).at[block_lists].add(value_contribution).astype(jnp.bfloat16)
    return (attended.reshape(TOKENS, HDIM), query_gradient.reshape(TOKENS, HDIM), key_grad.reshape(TOKENS, HDIM), value_grad.reshape(TOKENS, HDIM))

def reference(query_rows, key_rows, value_rows, out_grad, block_lists, block_counts):

    def by_head(array):
        return array.reshape(TOKENS, HEADS, HDIM).transpose(1, 0, 2)

    def one_head(operands):
        return head_pass(operands, block_lists, block_counts)
    results = lax.map(one_head, (by_head(query_rows), by_head(key_rows), by_head(value_rows), by_head(out_grad)))

    def back(array):
        return array.transpose(1, 0, 2).reshape(TOKENS, WIDTH)
    return (back(results[0]), back(results[1]), back(results[2]), back(results[3]))
```

```python
import functools
import math

import jax
import jax.numpy as jnp
from jax import lax
from jax.experimental import pallas as pl
from jax.experimental.pallas import tpu as pltpu
from jax.sharding import PartitionSpec as P

HDIM = 64
BLK = 64
KSEL = 8
PAIR = 2 * HDIM
SCALE = 1.0 / math.sqrt(HDIM)
GROUP = 16
MIB = 1024 * 1024
LANES = 128
LAG = 3


def dot(a, b, dims):
    return lax.dot_general(a, b, (dims, ((), ())), preferred_element_type=jnp.float32)


def attention_kernel(group, lists_hbm, counts_hbm, qd, kv, od, dkv, lists, counts, acc, sems):
    loads = (
        pltpu.make_async_copy(lists_hbm, lists, sems.at[0]),
        pltpu.make_async_copy(counts_hbm, counts, sems.at[1]),
    )
    for load in loads:
        load.start()
    for h in range(qd.shape[0]):
        acc[...] = jnp.zeros_like(acc)
        if h == 0:
            for load in loads:
                load.wait()
        attend_head(group, lists, counts, qd.at[h], kv.at[h], od.at[h], acc)
        dkv[h] = acc[...].astype(dkv.dtype)


def attend_head(group, lists, counts, qd_ref, kv_ref, od_ref, acc):
    local_blocks = qd_ref.shape[0] // BLK
    lane = lax.broadcasted_iota(jnp.int32, (BLK, PAIR), 1)
    first = lane < HDIM
    column = lax.broadcasted_iota(jnp.int32, (BLK, KSEL * BLK), 1)

    def one_block(b):
        rows = pl.ds(pl.multiple_of(b * BLK, BLK), BLK)
        picks = [pl.ds(pl.multiple_of(lists[j, b] * BLK, BLK), BLK) for j in range(KSEL)]
        qd = qd_ref[rows, :]
        zero = jnp.zeros_like(qd)
        diag = jnp.concatenate([jnp.where(first, qd * SCALE, zero), jnp.where(first, zero, qd)], axis=0)
        kv = jnp.concatenate([kv_ref[pick, :] for pick in picks], axis=0)
        both = dot(diag, kv, ((1,), (1,)))
        scores = jnp.where(column < counts[b] * BLK, both[:BLK], -1e30)
        weights = jnp.exp(scores - jnp.max(scores, axis=1, keepdims=True))
        prob = weights * (1.0 / jnp.sum(weights, axis=1, keepdims=True))
        rounded = prob.astype(jnp.bfloat16)
        delta = jnp.sum(rounded.astype(jnp.float32) * both[BLK:], axis=1, keepdims=True)
        grad_score = (prob * (both[BLK:] - delta)).astype(jnp.bfloat16)
        stacked = jnp.concatenate([grad_score, rounded], axis=0)
        rows_out = dot(stacked, kv, ((1,), (0,)))
        od_ref[rows, :] = jnp.where(first, rows_out[:BLK] * SCALE, rows_out[BLK:]).astype(jnp.bfloat16)
        terms = dot(stacked, diag, ((0,), (0,)))
        return picks, terms

    def turn(g, carry):
        done = [one_block(g * group + i) for i in range(group)]
        for picks, terms in done:
            for j, pick in enumerate(picks):
                acc[pick, :] += terms[j * BLK : (j + 1) * BLK]
        return carry

    lax.fori_loop(0, local_blocks // group, turn, 0)

def attention(block_lists, block_counts, qd, kv):
    heads_here, seg_rows, _ = qd.shape
    all_rows = kv.shape[1]
    vmem = pl.BlockSpec(memory_space=pltpu.VMEM)
    hbm = pl.BlockSpec(memory_space=pltpu.HBM)
    lists = block_lists.T
    limit = 6 * MIB + 4 * all_rows * PAIR + 4 * heads_here * (all_rows + seg_rows) * PAIR
    return pl.pallas_call(
        functools.partial(attention_kernel, math.gcd(GROUP, seg_rows // BLK)),
        out_shape=(
            jax.ShapeDtypeStruct(qd.shape, jnp.bfloat16),
            jax.ShapeDtypeStruct(kv.shape, jnp.bfloat16),
        ),
        in_specs=[hbm, hbm, vmem, vmem],
        out_specs=(vmem, vmem),
        scratch_shapes=[
            pltpu.SMEM(lists.shape, jnp.int32),
            pltpu.SMEM(block_counts.shape, jnp.int32),
            pltpu.VMEM((all_rows, PAIR), jnp.float32),
            pltpu.SemaphoreType.DMA((2,)),
        ],
        compiler_params=pltpu.CompilerParams(vmem_limit_bytes=limit),
        name="attention",
    )(
        pltpu.with_memory_space_constraint(lists, pltpu.HBM),
        pltpu.with_memory_space_constraint(block_counts, pltpu.HBM),
        qd,
        kv,
    )


MESH = pl.DeviceIdType.MESH


def places():
    seg, lane = lax.axis_index("blk"), lax.axis_index("uly")
    core = lax.rem(seg, 2)
    return seg, lane, seg + 1 - 2 * core, lax.rem(seg + 2, 4)


def remote(src, dst, send, recv, device):
    return pltpu.make_async_remote_copy(
        src_ref=src, dst_ref=dst, send_sem=send, recv_sem=recv, device_id=device, device_id_type=MESH
    )


def greet(lanes, diagonal=False):
    seg, lane, other, across = places()
    barrier = pltpu.get_barrier_semaphore()

    def one(i, carry):
        device = (seg, lax.rem(lane + i, lanes))
        pl.semaphore_signal(barrier, inc=1, device_id=device, device_id_type=MESH)
        return carry

    lax.fori_loop(1, lanes, one, 0)
    for near in (other, across, lax.rem(other + 2, 4))[: 3 if diagonal else 2]:
        pl.semaphore_signal(barrier, inc=1, device_id=(near, lane), device_id_type=MESH)
    return barrier


def loop(start, stop, body):
    lax.fori_loop(start, stop, lambda i, carry: (body(i), carry)[1], 0)


def join(left, right):
    return jnp.concatenate([left, right], axis=1)


def gather_kernel(
    lanes, q_hbm, k_hbm, v_hbm, g_hbm, qd, kv,
    k_ref, v_ref, q_ref, g_ref, qd_out, kv_out, in_s, qd_s, qd_r, kv_s, kv_r, x_s, x_r, c_s, c_r,
):
    pairs = ((k_hbm, k_ref), (v_hbm, v_ref), (q_hbm, q_ref), (g_hbm, g_ref))
    loads = [pltpu.make_async_copy(*pair, in_s.at[n]) for n, pair in enumerate(pairs)]
    for load in loads:
        load.start()
    seg, lane, other, across = places()
    heads_here = qd.shape[1]
    barrier = greet(lanes, True)

    def pack(left, right, to):
        for h in range(lanes * heads_here):
            columns = slice(h * HDIM, (h + 1) * HDIM)
            to[h // heads_here, h % heads_here] = join(left[:, columns], right[:, columns])

    loads[0].wait()
    loads[1].wait()
    pack(k_ref, v_ref, kv_out)
    pl.semaphore_wait(barrier, lanes + 2)

    def kv_copy(i, target, source):
        return remote(kv_out.at[target], kv.at[seg, source], kv_s.at[i], kv_r.at[i], (seg, target))

    def qd_copy(i, target, source):
        return remote(qd_out.at[target], qd.at[source], qd_s.at[i], qd_r.at[i], (seg, target))

    def x_copy(i, source, whose):
        return remote(kv.at[whose, source], kv.at[whose, source], x_s.at[i], x_r.at[i], (across, lane))

    def c_copy(n, i, source, whose):
        block = kv.at[whose, source]
        near = other if n == 0 else lax.rem(other + 2, 4)
        return remote(block, block, c_s.at[n, i], c_r.at[n, i], (near, lane))

    def ahead(i):
        return lax.rem(lane + i, lanes)

    def behind(i):
        return lax.rem(lane + lanes - i, lanes)

    loop(1, lanes, lambda i: kv_copy(i, ahead(i), lane).start())
    kv[seg, lane] = kv_out[lane]
    x_copy(0, lane, seg).start()
    c_copy(1, 0, lane, seg).start()
    c_copy(0, 0, lane, seg).start()
    loads[2].wait()
    loads[3].wait()
    pack(q_ref, g_ref, qd_out)
    qd[lane] = qd_out[lane]

    def arrive(i):
        kv_copy(i, lane, behind(i)).wait_recv()
        x_copy(i, behind(i), seg).start()
        qd_copy(i, ahead(i), lane).start()
        c_copy(1, i, behind(i), seg).start()
        c_copy(0, i, behind(i), seg).start()

    loop(1, lanes, arrive)
    loop(0, lanes, lambda i: x_copy(i, behind(i), across).wait_recv())

    def finish(i):
        c_copy(0, i, behind(i), other).wait_recv()
        c_copy(1, i, behind(i), lax.rem(other + 2, 4)).wait_recv()
        x_copy(i, behind(i), seg).wait_send()
        c_copy(0, i, behind(i), seg).wait_send()
        c_copy(1, i, behind(i), seg).wait_send()

    loop(0, lanes, finish)

    def finish_lanes(i):
        qd_copy(i, lane, behind(i)).wait_recv()
        qd_copy(i, ahead(i), lane).wait_send()
        kv_copy(i, ahead(i), lane).wait_send()

    loop(1, lanes, finish_lanes)


def return_kernel(
    lanes, od, dkv, od_in, end_in, core_in, x_out, x_in, end_out,
    od_s, od_r, c_s, c_r, x_s, x_r, e_s, e_r,
):
    seg, lane, other, across = places()
    heads_here = od.shape[1]
    barrier = greet(lanes)

    def ahead(i):
        return lax.rem(lane + i, lanes)

    def behind(i):
        return lax.rem(lane + lanes - i, lanes)

    def od_copy(i, target, source):
        return remote(od.at[target], od_in.at[source], od_s.at[i], od_r.at[i], (seg, target))

    def end_copy(i, target, source):
        return remote(end_out.at[target], end_in.at[source], e_s.at[i], e_r.at[i], (seg, target))

    def c_copy(n, i, whose):
        return remote(dkv.at[whose, ahead(i)], core_in.at[n, ahead(i)], c_s.at[n, i], c_r.at[n, i], (other, lane))

    def x_copy(i):
        return remote(x_out.at[ahead(i)], x_in.at[ahead(i)], x_s.at[i], x_r.at[i], (across, lane))

    def send(i):
        c_copy(1, i, lax.rem(other + 2, 4)).start()
        c_copy(0, i, other).start()

    def wide(block):
        return block.astype(jnp.float32)

    def reduce_core(i):
        c_copy(1, i, other).wait_recv()
        to = ahead(i)
        x_out[to] = (wide(dkv[across, to]) + wide(core_in[1, to])).astype(jnp.bfloat16)
        x_copy(i).start()

    def total(i):
        c_copy(0, i, other).wait_recv()
        x_copy(i).wait_recv()
        to = ahead(i)
        return (wide(dkv[seg, to]) + wide(core_in[0, to]) + wide(x_in[to])).astype(jnp.bfloat16)

    def reduce_chip(i):
        end_out[ahead(i)] = total(i)
        end_copy(i, ahead(i), lane).start()

    lag = min(4, lanes - 1)
    pl.semaphore_wait(barrier, lanes + 1)
    loop(1, lanes + 1, send)
    loop(1, lanes, lambda i: od_copy(i, ahead(i), lane).start())
    od_in[lane] = od[lane]
    loop(1, lag + 1, reduce_core)

    def both(i):
        reduce_core(i)
        reduce_chip(i - lag)

    loop(lag + 1, lanes + 1, both)
    loop(lanes + 1 - lag, lanes, reduce_chip)
    end_in[lane] = total(lanes)

    def finish(i):
        c_copy(0, i, other).wait_send()
        c_copy(1, i, other).wait_send()
        x_copy(i).wait_send()

    loop(1, lanes + 1, finish)

    def finish_lanes(i):
        od_copy(i, lane, behind(i)).wait_recv()
        end_copy(i, lane, behind(i)).wait_recv()
        od_copy(i, ahead(i), lane).wait_send()
        end_copy(i, ahead(i), lane).wait_send()

    loop(1, lanes, finish_lanes)


def exchange(lanes, lane, i):
    flips, partner, bit = lanes - 1 - i, 0, 1
    while bit < lanes:
        partner += bit * lax.rem(lax.div(lane, bit) + flips // bit, 2)
        bit *= 2
    return partner


def block_diagonal(qd):
    first = lax.broadcasted_iota(jnp.int32, qd.shape, 1) < HDIM
    zero = jnp.zeros_like(qd)
    return jnp.concatenate([jnp.where(first, qd * SCALE, zero), jnp.where(first, zero, qd)], axis=0)


def block_rows(b):
    return pl.ds(pl.multiple_of(b * BLK, BLK), BLK)


def seen_rows(kv, lists, b):
    return jnp.concatenate([kv[lists[j, b]] for j in range(KSEL)], axis=0)


def score_block(qd, kv, lists, b, both):
    both[...] = dot(block_diagonal(qd[block_rows(b), :]), seen_rows(kv, lists, b), ((1,), (1,)))


def softmax_block(counts, b, both, stacked):
    column = lax.broadcasted_iota(jnp.int32, (1, KSEL * BLK), 1)
    scores = jnp.where(column < counts[b] * BLK, both[:BLK, :], -1e30)
    weights = jnp.exp(scores - jnp.max(scores, axis=1, keepdims=True))
    prob = weights * (1.0 / jnp.sum(weights, axis=1, keepdims=True))
    stacked[BLK:, :] = prob.astype(jnp.bfloat16)
    grad_prob = both[BLK:, :]
    delta = jnp.sum(prob * grad_prob, axis=1, keepdims=True)
    stacked[:BLK, :] = (prob * (grad_prob - delta)).astype(jnp.bfloat16)


def gradient_block(qd, kv, lists, chain, b, slot, stacked, od, sums):
    first = lax.broadcasted_iota(jnp.int32, (BLK, PAIR), 1) < HDIM
    both = stacked[...]
    rows_out = dot(both, seen_rows(kv, lists, b), ((1,), (0,)))
    od[block_rows(b), :] = jnp.where(first, rows_out[:BLK] * SCALE, rows_out[BLK:]).astype(jnp.bfloat16)
    terms = dot(both, block_diagonal(qd[block_rows(b), :]), ((0,), (0,)))
    for j in range(KSEL):
        before = sums[chain[0, j * (LANES // KSEL) + b]]
        sums[slot + j] = before + terms[j * BLK : (j + 1) * BLK]


def link_terms(lanes, seg, lane, lists, out):
    blocks = 2 * lanes

    def iota(shape, axis):
        return lax.broadcasted_iota(jnp.int32, shape, axis)

    def parts(axis):
        entry = iota((LANES, LANES), axis)
        j, b = lax.div(entry, blocks), lax.rem(entry, blocks)
        turn = lanes - 1 - jnp.bitwise_xor(lax.div(b, 2), lane)
        return j, b, 2 * turn + lax.rem(b, 2)

    wide = jnp.concatenate([lists[...]] * (LANES // blocks), axis=1)
    own_row = iota((KSEL, LANES), 0) == lax.div(iota((KSEL, LANES), 1), blocks)
    row = jnp.sum(jnp.where(own_row, wide, 0), axis=0, keepdims=True)
    across = jnp.broadcast_to(row, (LANES, LANES))
    down = across.T
    j, b, when = parts(0)
    now = parts(1)[2]
    slot = KSEL * when + j
    valid = jnp.logical_or(j == 0, down != seg * blocks + b)
    earlier = jnp.logical_and(jnp.logical_and(down == across, when < now), valid)
    same = jnp.logical_and(down == iota((LANES, LANES), 1), valid)
    for n, chosen in enumerate((earlier, same)):
        latest = jnp.max(jnp.where(chosen, slot, -1), axis=0, keepdims=True)
        out[n : n + 1, :] = jnp.where(latest < 0, LANES, latest)


def fused_kernel(
    lanes, q_hbm, k_hbm, v_hbm, g_hbm, lists_hbm, counts_hbm, od_in, end_in,
    k_ref, v_ref, q_ref, g_ref, qd_out, kv_out, qd, kv, od, sums, both, stacked,
    core_out, core_in, x_out, x_in, end_out, lists, counts, lists_v, chain_v, chain,
    in_s, idx_s, kv_s, kv_r, qd_s, qd_r, x_s, x_r, c_s, c_r, od_s, od_r, e_s, e_r, dx_s, dx_r, dc_s, dc_r,
):
    rows = q_hbm.shape[0]
    own = lanes - 1
    pairs = (
        (k_hbm, k_ref), (v_hbm, v_ref), (q_hbm, q_ref), (g_hbm, g_ref),
        (lists_hbm, lists_v), (lists_hbm, lists), (counts_hbm, counts),
    )
    loads = [pltpu.make_async_copy(*pair, in_s.at[n]) for n, pair in enumerate(pairs)]
    for load in loads:
        load.start()
    seg, lane, other, across = places()
    beyond = lax.rem(other + 2, 4)
    barrier = greet(lanes)

    def source(i):
        return exchange(lanes, lane, i)

    def pack(left, right, to):
        for h in range(lanes):
            columns = slice(h * HDIM, (h + 1) * HDIM)
            to[h] = join(left[:, columns], right[:, columns]).reshape(to.shape[1:])

    def chunk(i):
        return pl.ds(pl.multiple_of(i * rows, rows), rows)

    def piece(whose, i):
        return kv.at[pl.ds(2 * (whose * lanes + i), 2)]

    def kv_copy(i, target, whose):
        return remote(kv_out.at[target], piece(seg, whose), kv_s.at[i], kv_r.at[i], (seg, target))

    def qd_copy(i, target, whose):
        return remote(qd_out.at[target], qd.at[chunk(whose), :], qd_s.at[i], qd_r.at[i], (seg, target))

    def x_copy(i, whose):
        block = piece(whose, source(i))
        return remote(block, block, x_s.at[i], x_r.at[i], (across, lane))

    def c_copy(n, i, whose):
        block = piece(whose, source(i))
        return remote(block, block, c_s.at[n, i], c_r.at[n, i], (other, lane))

    def od_copy(i, target, whose):
        return remote(od.at[chunk(target), :], od_in.at[whose, 0], od_s.at[i], od_r.at[i], (seg, target))

    loads[0].wait()
    loads[1].wait()
    pack(k_ref, v_ref, kv_out)
    pl.semaphore_wait(barrier, lanes + 1)
    loop(0, own, lambda i: kv_copy(i, source(i), lane).start())
    kv[pl.ds(2 * (seg * lanes + lane), 2)] = kv_out[lane]
    x_copy(own, seg).start()
    c_copy(0, own, seg).start()
    loads[2].wait()
    loads[3].wait()
    pack(q_ref, g_ref, qd_out)
    qd[chunk(lane), :] = qd_out[lane]
    loads[4].wait()
    link_terms(lanes, seg, lane, lists_v, chain_v)
    chain_copy = pltpu.make_async_copy(chain_v, chain, idx_s.at[0])
    chain_copy.start()
    sums[LANES] = jnp.zeros((BLK, PAIR), jnp.float32)

    def forward(i):
        x_copy(i, across).wait_recv()
        c_copy(1, i, across).start()

    def arrive(i):
        kv_copy(i, source(i), source(i)).wait_recv()
        x_copy(i, seg).start()
        c_copy(0, i, seg).start()

    def send_qd(i):
        qd_copy(i, source(i), lane).start()

    def arrive_and_forward(i):
        arrive(i)
        forward(lax.rem(i + own, lanes))

    def arrive_and_send(i):
        arrive_and_forward(i)
        send_qd(i - LAG)

    loop(0, LAG, arrive_and_forward)
    loop(LAG, own, arrive_and_send)
    loop(own - LAG, own, send_qd)
    forward(own - 1)

    def complete(i):
        c_copy(0, i, other).wait_recv()
        c_copy(1, i, beyond).wait_recv()

    loop(0, lanes, complete)
    loads[5].wait()
    loads[6].wait()
    chain_copy.wait()

    def score(i, slot):
        for n in range(2):
            score_block(qd, kv, lists, 2 * source(i) + n, both.at[slot, n])

    def softmax(i, slot):
        for n in range(2):
            softmax_block(counts, 2 * source(i) + n, both.at[slot, n], stacked.at[slot, n])

    def gradient(i, slot):
        for n in range(2):
            gradient_block(
                qd, kv, lists, chain, 2 * source(i) + n, (2 * i + n) * KSEL, stacked.at[slot, n], od, sums
            )

    def receive_qd(i):
        qd_copy(i, source(i), source(i)).wait_recv()

    def send_od(i):
        od_copy(i, source(i), lane).start()

    receive_qd(0)
    score(0, 0)
    receive_qd(1)
    softmax(0, 0)
    score(1, 1)

    def two_steps(i, last):
        receive_qd(i)
        gradient(i - 2, 0)
        softmax(i - 1, 1)
        score(i, 0)
        send_od(i - 2)
        if not last:
            receive_qd(i + 1)
        gradient(i - 1, 1)
        softmax(i, 0)
        score(i + 1, 1)
        send_od(i - 1)

    loop(1, lanes // 2 - 1, lambda k: two_steps(2 * k, False))
    two_steps(lanes - 2, True)
    gradient(lanes - 2, 0)
    softmax(own, 1)
    send_od(lanes - 2)
    gradient(own, 1)
    od_in[lane, 0] = od[chunk(lane), :]

    def partial(whose, i):
        block = 2 * (whose * lanes + source(i))
        return jnp.concatenate([sums[chain[1, block + n]] for n in range(2)], axis=0)

    def dc_copy(n, i):
        return remote(core_out.at[n, i], core_in.at[n, i], dc_s.at[n, i], dc_r.at[n, i], (other, lane))

    def dx_copy(i):
        return remote(x_out.at[i], x_in.at[i], dx_s.at[i], dx_r.at[i], (across, lane))

    def end_copy(i, target, whose):
        return remote(end_out.at[i], end_in.at[whose, 0], e_s.at[i], e_r.at[i], (seg, target))

    def to_core(n, i, whose):
        core_out[n, i] = partial(whose, i).astype(jnp.bfloat16)
        dc_copy(n, i).start()

    def to_chip(i):
        dc_copy(1, i).wait_recv()
        x_out[i] = (partial(across, i) + core_in[1, i].astype(jnp.float32)).astype(jnp.bfloat16)
        dx_copy(i).start()
        to_core(0, i, other)

    def total(i):
        mine = partial(seg, i)
        dc_copy(0, i).wait_recv()
        dx_copy(i).wait_recv()
        near = core_in[0, i].astype(jnp.float32)
        return (mine + near + x_in[i].astype(jnp.float32)).astype(jnp.bfloat16)

    def to_owner(i):
        end_out[i] = total(i)
        end_copy(i, source(i), lane).start()

    loop(0, lanes, lambda i: to_core(1, i, beyond))
    loop(0, lanes, to_chip)
    loop(0, own, to_owner)
    end_in[lane, 0] = total(own)

    def finish(i):
        for n in range(2):
            c_copy(n, i, seg).wait_send()
            dc_copy(n, i).wait_send()
        x_copy(i, seg).wait_send()
        dx_copy(i).wait_send()

    loop(0, lanes, finish)

    def finish_lanes(i):
        kv_copy(i, source(i), lane).wait_send()
        qd_copy(i, source(i), lane).wait_send()
        od_copy(i, source(i), lane).wait_send()
        od_copy(i, source(i), source(i)).wait_recv()
        end_copy(i, source(i), lane).wait_send()
        end_copy(i, source(i), source(i)).wait_recv()

    loop(0, own, finish_lanes)


def fits(lanes, heads_here, rows):
    return heads_here == 1 and rows == 2 * BLK and 2 * lanes * KSEL == LANES


def fused(lanes, query_rows, key_rows, value_rows, out_grad, block_lists, block_counts):
    rows, width = query_rows.shape
    segs, half, f32 = 4, jnp.bfloat16, jnp.float32
    vmem = pl.BlockSpec(memory_space=pltpu.VMEM)
    hbm = pl.BlockSpec(memory_space=pltpu.HBM)
    dma = pltpu.SemaphoreType.DMA
    lists = block_lists.T
    chunks = (lanes, rows, PAIR)
    buffers = (
        [((rows, width), half)] * 4
        + [(chunks, half), ((lanes, 2, BLK, PAIR), half)]
        + [((lanes * rows, PAIR), half), ((2 * segs * lanes, BLK, PAIR), half), ((lanes * rows, PAIR), half)]
        + [((LANES + 1, BLK, PAIR), f32)]
        + [((2, 2, 2 * BLK, KSEL * BLK), f32), ((2, 2, 2 * BLK, KSEL * BLK), half)]
        + [((2, *chunks), half)] * 2
        + [(chunks, half)] * 3
    )
    size = sum(math.prod(shape) * jnp.dtype(kind).itemsize for shape, kind in buffers)
    return pl.pallas_call(
        functools.partial(fused_kernel, lanes),
        out_shape=[jax.ShapeDtypeStruct((lanes, 1, rows, PAIR), half)] * 2,
        in_specs=[hbm] * 6,
        out_specs=[vmem] * 2,
        scratch_shapes=[pltpu.VMEM(*buffer) for buffer in buffers]
        + [pltpu.SMEM(lists.shape, jnp.int32), pltpu.SMEM(block_counts.shape, jnp.int32)]
        + [pltpu.VMEM(lists.shape, jnp.int32), pltpu.VMEM((8, LANES), jnp.int32), pltpu.SMEM((8, LANES), jnp.int32)]
        + [dma((7,)), dma((1,))]
        + [dma((lanes,))] * 6
        + [dma((2, lanes))] * 2
        + [dma((lanes,))] * 6
        + [dma((2, lanes))] * 2,
        compiler_params=pltpu.CompilerParams(
            collective_id=0, has_side_effects=True, vmem_limit_bytes=6 * MIB + size + 4 * lanes * rows * PAIR
        ),
        name="fused",
    )(
        *(
            pltpu.with_memory_space_constraint(a, pltpu.HBM)
            for a in (query_rows, key_rows, value_rows, out_grad, lists, block_counts)
        )
    )


def unpack_kernel(od, dkv, out_ref, dq_ref, dk_ref, dv_ref):
    for block, left, right in ((od, dq_ref, out_ref), (dkv, dk_ref, dv_ref)):
        heads_here = block.shape[1]
        for h in range(0, block.shape[0] * heads_here, 2):
            a, b = (block[g // heads_here, g % heads_here] for g in (h, h + 1))
            columns = slice(h * HDIM, (h + 2) * HDIM)
            left[:, columns] = join(a[:, :HDIM], b[:, :HDIM])
            right[:, columns] = join(a[:, HDIM:], b[:, HDIM:])


def comm_params(number, chunks, block):
    chunk_bytes = 2 * math.prod(block)
    return pltpu.CompilerParams(
        collective_id=number, has_side_effects=True, vmem_limit_bytes=4 * MIB + chunks * chunk_bytes
    )


def staged(lanes, query_rows, key_rows, value_rows, out_grad, block_lists, block_counts):
    rows, width = query_rows.shape
    heads_here = width // HDIM // lanes
    segs = 4
    block = (heads_here, rows, PAIR)
    vmem = pl.BlockSpec(memory_space=pltpu.VMEM)
    dma = pltpu.SemaphoreType.DMA
    half = jnp.bfloat16
    chunks = jax.ShapeDtypeStruct((lanes, *block), half)

    qd, kv = pl.pallas_call(
        functools.partial(gather_kernel, lanes),
        out_shape=(chunks, jax.ShapeDtypeStruct((segs, lanes, *block), half)),
        in_specs=[pl.BlockSpec(memory_space=pltpu.HBM)] * 4,
        out_specs=(vmem, vmem),
        scratch_shapes=[pltpu.VMEM((rows, width), half)] * 4
        + [pltpu.VMEM((lanes, *block), half)] * 2
        + [dma((4,))]
        + [dma((lanes,))] * 6
        + [dma((2, lanes))] * 2,
        compiler_params=comm_params(0, 10 * lanes, block),
        name="gather",
    )(*(pltpu.with_memory_space_constraint(a, pltpu.HBM) for a in (query_rows, key_rows, value_rows, out_grad)))

    qd = qd.transpose(1, 0, 2, 3).reshape(heads_here, lanes * rows, PAIR)
    kv = kv.transpose(2, 0, 1, 3, 4).reshape(heads_here, segs * lanes * rows, PAIR)
    od, dkv = attention(block_lists, block_counts, qd, kv)
    od = od.reshape(heads_here, lanes, rows, PAIR).transpose(1, 0, 2, 3)
    dkv = dkv.reshape(heads_here, segs, lanes, rows, PAIR).transpose(1, 2, 0, 3, 4)

    od, dkv = pl.pallas_call(
        functools.partial(return_kernel, lanes),
        out_shape=[chunks] * 2,
        in_specs=[vmem] * 2,
        out_specs=[vmem] * 2,
        scratch_shapes=[pltpu.VMEM((2, lanes, *block), half)]
        + [pltpu.VMEM((lanes, *block), half)] * 3
        + [dma((lanes + 1,))] * 2
        + [dma((2, lanes + 1))] * 2
        + [dma((lanes + 1,))] * 4,
        compiler_params=comm_params(1, 14 * lanes, block),
        name="scatter",
    )(od, dkv)

    return od, dkv


def on_device(lanes, *arrays):
    rows, width = arrays[0].shape
    half = jnp.bfloat16
    vmem = pl.BlockSpec(memory_space=pltpu.VMEM)
    gather = fused if fits(lanes, width // HDIM // lanes, rows) else staged
    od, dkv = gather(lanes, *arrays)
    return pl.pallas_call(
        unpack_kernel,
        out_shape=[jax.ShapeDtypeStruct((rows, width), half)] * 4,
        in_specs=[vmem] * 2,
        out_specs=[vmem] * 4,
        compiler_params=pltpu.CompilerParams(vmem_limit_bytes=4 * MIB + 32 * rows * width),
        name="unpack",
    )(od, dkv)


def solution(mesh):
    tokens = P(("blk", "uly"), None)
    return jax.shard_map(
        functools.partial(on_device, mesh.shape["uly"]),
        mesh=mesh,
        in_specs=(tokens, tokens, tokens, tokens, P("blk", None), P("blk")),
        out_specs=(tokens, tokens, tokens, tokens),
        check_vma=False,
    )
```

```python
import functools
import math

import jax
import jax.numpy as jnp
from jax import lax
from jax.experimental import pallas as pl
from jax.experimental.pallas import tpu as pltpu
from jax.sharding import PartitionSpec as P

HDIM = 64
BLK = 64
KSEL = 8
PAIR = 2 * HDIM
SCALE = 1.0 / math.sqrt(HDIM)
GROUP = 16
MIB = 1024 * 1024
LANES = 128


def dot(a, b, dims):
    return lax.dot_general(a, b, (dims, ((), ())), preferred_element_type=jnp.float32)


def attention_kernel(group, lists_hbm, counts_hbm, qd, kv, od, dkv, lists, counts, acc, sems):
    loads = (
        pltpu.make_async_copy(lists_hbm, lists, sems.at[0]),
        pltpu.make_async_copy(counts_hbm, counts, sems.at[1]),
    )
    for load in loads:
        load.start()
    for h in range(qd.shape[0]):
        acc[...] = jnp.zeros_like(acc)
        if h == 0:
            for load in loads:
                load.wait()
        attend_head(group, lists, counts, qd.at[h], kv.at[h], od.at[h], acc)
        dkv[h] = acc[...].astype(dkv.dtype)


def attend_head(group, lists, counts, qd_ref, kv_ref, od_ref, acc):
    local_blocks = qd_ref.shape[0] // BLK
    lane = lax.broadcasted_iota(jnp.int32, (BLK, PAIR), 1)
    first = lane < HDIM
    column = lax.broadcasted_iota(jnp.int32, (BLK, KSEL * BLK), 1)

    def one_block(b):
        rows = pl.ds(pl.multiple_of(b * BLK, BLK), BLK)
        picks = [pl.ds(pl.multiple_of(lists[j, b] * BLK, BLK), BLK) for j in range(KSEL)]
        qd = qd_ref[rows, :]
        zero = jnp.zeros_like(qd)
        diag = jnp.concatenate([jnp.where(first, qd * SCALE, zero), jnp.where(first, zero, qd)], axis=0)
        kv = jnp.concatenate([kv_ref[pick, :] for pick in picks], axis=0)
        both = dot(diag, kv, ((1,), (1,)))
        scores = jnp.where(column < counts[b] * BLK, both[:BLK], -1e30)
        weights = jnp.exp(scores - jnp.max(scores, axis=1, keepdims=True))
        prob = weights * (1.0 / jnp.sum(weights, axis=1, keepdims=True))
        rounded = prob.astype(jnp.bfloat16)
        delta = jnp.sum(rounded.astype(jnp.float32) * both[BLK:], axis=1, keepdims=True)
        grad_score = (prob * (both[BLK:] - delta)).astype(jnp.bfloat16)
        stacked = jnp.concatenate([grad_score, rounded], axis=0)
        rows_out = dot(stacked, kv, ((1,), (0,)))
        od_ref[rows, :] = jnp.where(first, rows_out[:BLK] * SCALE, rows_out[BLK:]).astype(jnp.bfloat16)
        terms = dot(stacked, diag, ((0,), (0,)))
        return picks, terms

    def turn(g, carry):
        done = [one_block(g * group + i) for i in range(group)]
        for picks, terms in done:
            for j, pick in enumerate(picks):
                acc[pick, :] += terms[j * BLK : (j + 1) * BLK]
        return carry

    lax.fori_loop(0, local_blocks // group, turn, 0)

def attention(block_lists, block_counts, qd, kv):
    heads_here, seg_rows, _ = qd.shape
    all_rows = kv.shape[1]
    vmem = pl.BlockSpec(memory_space=pltpu.VMEM)
    hbm = pl.BlockSpec(memory_space=pltpu.HBM)
    lists = block_lists.T
    limit = 6 * MIB + 4 * all_rows * PAIR + 4 * heads_here * (all_rows + seg_rows) * PAIR
    return pl.pallas_call(
        functools.partial(attention_kernel, math.gcd(GROUP, seg_rows // BLK)),
        out_shape=(
            jax.ShapeDtypeStruct(qd.shape, jnp.bfloat16),
            jax.ShapeDtypeStruct(kv.shape, jnp.bfloat16),
        ),
        in_specs=[hbm, hbm, vmem, vmem],
        out_specs=(vmem, vmem),
        scratch_shapes=[
            pltpu.SMEM(lists.shape, jnp.int32),
            pltpu.SMEM(block_counts.shape, jnp.int32),
            pltpu.VMEM((all_rows, PAIR), jnp.float32),
            pltpu.SemaphoreType.DMA((2,)),
        ],
        compiler_params=pltpu.CompilerParams(vmem_limit_bytes=limit),
        name="attention",
    )(
        pltpu.with_memory_space_constraint(lists, pltpu.HBM),
        pltpu.with_memory_space_constraint(block_counts, pltpu.HBM),
        qd,
        kv,
    )


MESH = pl.DeviceIdType.MESH


def places():
    seg, lane = lax.axis_index("blk"), lax.axis_index("uly")
    core = lax.rem(seg, 2)
    return seg, lane, seg + 1 - 2 * core, lax.rem(seg + 2, 4)


def remote(src, dst, send, recv, device):
    return pltpu.make_async_remote_copy(
        src_ref=src, dst_ref=dst, send_sem=send, recv_sem=recv, device_id=device, device_id_type=MESH
    )


def greet(lanes, diagonal=False):
    seg, lane, other, across = places()
    barrier = pltpu.get_barrier_semaphore()

    def one(i, carry):
        device = (seg, lax.rem(lane + i, lanes))
        pl.semaphore_signal(barrier, inc=1, device_id=device, device_id_type=MESH)
        return carry

    lax.fori_loop(1, lanes, one, 0)
    for near in (other, across, lax.rem(other + 2, 4))[: 3 if diagonal else 2]:
        pl.semaphore_signal(barrier, inc=1, device_id=(near, lane), device_id_type=MESH)
    return barrier


def loop(start, stop, body):
    lax.fori_loop(start, stop, lambda i, carry: (body(i), carry)[1], 0)


def join(left, right):
    return jnp.concatenate([left, right], axis=1)


def gather_kernel(
    lanes, q_hbm, k_hbm, v_hbm, g_hbm, qd, kv,
    k_ref, v_ref, q_ref, g_ref, qd_out, kv_out, in_s, qd_s, qd_r, kv_s, kv_r, x_s, x_r, c_s, c_r,
):
    pairs = ((k_hbm, k_ref), (v_hbm, v_ref), (q_hbm, q_ref), (g_hbm, g_ref))
    loads = [pltpu.make_async_copy(*pair, in_s.at[n]) for n, pair in enumerate(pairs)]
    for load in loads:
        load.start()
    seg, lane, other, across = places()
    heads_here = qd.shape[1]
    barrier = greet(lanes, True)

    def pack(left, right, to):
        for h in range(lanes * heads_here):
            columns = slice(h * HDIM, (h + 1) * HDIM)
            to[h // heads_here, h % heads_here] = join(left[:, columns], right[:, columns])

    loads[0].wait()
    loads[1].wait()
    pack(k_ref, v_ref, kv_out)
    pl.semaphore_wait(barrier, lanes + 2)

    def kv_copy(i, target, source):
        return remote(kv_out.at[target], kv.at[seg, source], kv_s.at[i], kv_r.at[i], (seg, target))

    def qd_copy(i, target, source):
        return remote(qd_out.at[target], qd.at[source], qd_s.at[i], qd_r.at[i], (seg, target))

    def x_copy(i, source, whose):
        return remote(kv.at[whose, source], kv.at[whose, source], x_s.at[i], x_r.at[i], (across, lane))

    def c_copy(n, i, source, whose):
        block = kv.at[whose, source]
        near = other if n == 0 else lax.rem(other + 2, 4)
        return remote(block, block, c_s.at[n, i], c_r.at[n, i], (near, lane))

    def ahead(i):
        return lax.rem(lane + i, lanes)

    def behind(i):
        return lax.rem(lane + lanes - i, lanes)

    loop(1, lanes, lambda i: kv_copy(i, ahead(i), lane).start())
    kv[seg, lane] = kv_out[lane]
    x_copy(0, lane, seg).start()
    c_copy(1, 0, lane, seg).start()
    c_copy(0, 0, lane, seg).start()
    loads[2].wait()
    loads[3].wait()
    pack(q_ref, g_ref, qd_out)
    qd[lane] = qd_out[lane]

    def arrive(i):
        kv_copy(i, lane, behind(i)).wait_recv()
        x_copy(i, behind(i), seg).start()
        qd_copy(i, ahead(i), lane).start()
        c_copy(1, i, behind(i), seg).start()
        c_copy(0, i, behind(i), seg).start()

    loop(1, lanes, arrive)
    loop(0, lanes, lambda i: x_copy(i, behind(i), across).wait_recv())

    def finish(i):
        c_copy(0, i, behind(i), other).wait_recv()
        c_copy(1, i, behind(i), lax.rem(other + 2, 4)).wait_recv()
        x_copy(i, behind(i), seg).wait_send()
        c_copy(0, i, behind(i), seg).wait_send()
        c_copy(1, i, behind(i), seg).wait_send()

    loop(0, lanes, finish)

    def finish_lanes(i):
        qd_copy(i, lane, behind(i)).wait_recv()
        qd_copy(i, ahead(i), lane).wait_send()
        kv_copy(i, ahead(i), lane).wait_send()

    loop(1, lanes, finish_lanes)


def return_kernel(
    lanes, od, dkv, od_in, end_in, core_in, x_out, x_in, end_out,
    od_s, od_r, c_s, c_r, x_s, x_r, e_s, e_r,
):
    seg, lane, other, across = places()
    heads_here = od.shape[1]
    barrier = greet(lanes)

    def ahead(i):
        return lax.rem(lane + i, lanes)

    def behind(i):
        return lax.rem(lane + lanes - i, lanes)

    def od_copy(i, target, source):
        return remote(od.at[target], od_in.at[source], od_s.at[i], od_r.at[i], (seg, target))

    def end_copy(i, target, source):
        return remote(end_out.at[target], end_in.at[source], e_s.at[i], e_r.at[i], (seg, target))

    def c_copy(n, i, whose):
        return remote(dkv.at[whose, ahead(i)], core_in.at[n, ahead(i)], c_s.at[n, i], c_r.at[n, i], (other, lane))

    def x_copy(i):
        return remote(x_out.at[ahead(i)], x_in.at[ahead(i)], x_s.at[i], x_r.at[i], (across, lane))

    def send(i):
        c_copy(1, i, lax.rem(other + 2, 4)).start()
        c_copy(0, i, other).start()

    def wide(block):
        return block.astype(jnp.float32)

    def reduce_core(i):
        c_copy(1, i, other).wait_recv()
        to = ahead(i)
        x_out[to] = (wide(dkv[across, to]) + wide(core_in[1, to])).astype(jnp.bfloat16)
        x_copy(i).start()

    def total(i):
        c_copy(0, i, other).wait_recv()
        x_copy(i).wait_recv()
        to = ahead(i)
        return (wide(dkv[seg, to]) + wide(core_in[0, to]) + wide(x_in[to])).astype(jnp.bfloat16)

    def reduce_chip(i):
        end_out[ahead(i)] = total(i)
        end_copy(i, ahead(i), lane).start()

    lag = min(4, lanes - 1)
    pl.semaphore_wait(barrier, lanes + 1)
    loop(1, lanes + 1, send)
    loop(1, lanes, lambda i: od_copy(i, ahead(i), lane).start())
    od_in[lane] = od[lane]
    loop(1, lag + 1, reduce_core)

    def both(i):
        reduce_core(i)
        reduce_chip(i - lag)

    loop(lag + 1, lanes + 1, both)
    loop(lanes + 1 - lag, lanes, reduce_chip)
    end_in[lane] = total(lanes)

    def finish(i):
        c_copy(0, i, other).wait_send()
        c_copy(1, i, other).wait_send()
        x_copy(i).wait_send()

    loop(1, lanes + 1, finish)

    def finish_lanes(i):
        od_copy(i, lane, behind(i)).wait_recv()
        end_copy(i, lane, behind(i)).wait_recv()
        od_copy(i, ahead(i), lane).wait_send()
        end_copy(i, ahead(i), lane).wait_send()

    loop(1, lanes, finish_lanes)


def exchange(lanes, lane, m):
    partner, bit = 0, 1
    while bit < lanes:
        partner += bit * lax.rem(lax.div(lane, bit) + m // bit, 2)
        bit *= 2
    return partner


def chunk_at(lanes, n):
    return lax.rem(n + 1, 2) * (lanes - 1 - n // 2) + lax.rem(n, 2) * (n // 2)


def block_diagonal(qd):
    first = lax.broadcasted_iota(jnp.int32, qd.shape, 1) < HDIM
    zero = jnp.zeros_like(qd)
    return jnp.concatenate([jnp.where(first, qd * SCALE, zero), jnp.where(first, zero, qd)], axis=0)


def block_rows(b):
    return pl.ds(pl.multiple_of(b * BLK, BLK), BLK)


def seen_rows(kv, lists, b):
    return jnp.concatenate([kv[lists[j, b]] for j in range(KSEL)], axis=0)


def score_block(qd, kv, lists, b, both):
    both[...] = dot(block_diagonal(qd[block_rows(b), :]), seen_rows(kv, lists, b), ((1,), (1,)))


def softmax_block(counts, b, both, stacked):
    column = lax.broadcasted_iota(jnp.int32, (1, KSEL * BLK), 1)
    scores = jnp.where(column < counts[b] * BLK, both[:BLK, :], -1e30)
    weights = jnp.exp(scores - jnp.max(scores, axis=1, keepdims=True))
    prob = weights * (1.0 / jnp.sum(weights, axis=1, keepdims=True))
    stacked[BLK:, :] = prob.astype(jnp.bfloat16)
    grad_prob = both[BLK:, :]
    delta = jnp.sum(prob * grad_prob, axis=1, keepdims=True)
    stacked[:BLK, :] = (prob * (grad_prob - delta)).astype(jnp.bfloat16)


def gradient_block(qd, kv, lists, chain, b, slot, stacked, od, sums):
    first = lax.broadcasted_iota(jnp.int32, (BLK, PAIR), 1) < HDIM
    both = stacked[...]
    rows_out = dot(both, seen_rows(kv, lists, b), ((1,), (0,)))
    od[block_rows(b), :] = jnp.where(first, rows_out[:BLK] * SCALE, rows_out[BLK:]).astype(jnp.bfloat16)
    terms = dot(both, block_diagonal(qd[block_rows(b), :]), ((0,), (0,)))
    for j in range(KSEL):
        before = sums[chain[0, j * (LANES // KSEL) + b]]
        sums[slot + j] = before + terms[j * BLK : (j + 1) * BLK]


def link_terms(lanes, seg, lane, lists, out):
    blocks = 2 * lanes

    def iota(shape, axis):
        return lax.broadcasted_iota(jnp.int32, shape, axis)

    def parts(axis):
        entry = iota((LANES, LANES), axis)
        j, b = lax.div(entry, blocks), lax.rem(entry, blocks)
        m = jnp.bitwise_xor(lax.div(b, 2), lane)
        turn = jnp.where(m < lanes // 2, 2 * m + 1, 2 * (lanes - 1 - m))
        return j, b, 2 * turn + lax.rem(b, 2)

    wide = jnp.concatenate([lists[...]] * (LANES // blocks), axis=1)
    own_row = iota((KSEL, LANES), 0) == lax.div(iota((KSEL, LANES), 1), blocks)
    row = jnp.sum(jnp.where(own_row, wide, 0), axis=0, keepdims=True)
    across = jnp.broadcast_to(row, (LANES, LANES))
    down = across.T
    j, b, when = parts(0)
    now = parts(1)[2]
    slot = KSEL * when + j
    valid = jnp.logical_or(j == 0, down != seg * blocks + b)
    earlier = jnp.logical_and(jnp.logical_and(down == across, when < now), valid)
    same = jnp.logical_and(down == iota((LANES, LANES), 1), valid)
    for n, chosen in enumerate((earlier, same)):
        latest = jnp.max(jnp.where(chosen, slot, -1), axis=0, keepdims=True)
        out[n : n + 1, :] = jnp.where(latest < 0, LANES, latest)


def fused_kernel(
    lanes, q_hbm, k_hbm, v_hbm, g_hbm, lists_hbm, counts_hbm, od_in, end_in,
    k_ref, v_ref, q_ref, g_ref, qd_out, kv_out, qd, kv, od, sums, both, stacked,
    core_out, core_in, x_out, x_in, end_out, lists, counts, lists_v, chain_v, chain,
    in_s, idx_s, kv_s, kv_r, qd_s, qd_r, x_s, x_r, c_s, c_r, od_s, od_r, e_s, e_r, dx_s, dx_r, dc_s, dc_r,
):
    rows = q_hbm.shape[0]
    half = lanes // 2
    pairs = (
        (k_hbm, k_ref), (v_hbm, v_ref), (q_hbm, q_ref), (g_hbm, g_ref),
        (lists_hbm, lists_v), (lists_hbm, lists), (counts_hbm, counts),
    )
    loads = [pltpu.make_async_copy(*pair, in_s.at[n]) for n, pair in enumerate(pairs)]
    for load in loads:
        load.start()
    seg, lane, other, across = places()
    beyond = lax.rem(other + 2, 4)
    barrier = greet(lanes)

    def at(m):
        return exchange(lanes, lane, m)

    def pack(left, right, to):
        for h in range(lanes):
            columns = slice(h * HDIM, (h + 1) * HDIM)
            to[h] = join(left[:, columns], right[:, columns]).reshape(to.shape[1:])

    def chunk(i):
        return pl.ds(pl.multiple_of(i * rows, rows), rows)

    def piece(whose, i):
        return kv.at[pl.ds(2 * (whose * lanes + i), 2)]

    def kv_copy(m, whose):
        return remote(kv_out.at[at(m)], piece(seg, whose), kv_s.at[m], kv_r.at[m], (seg, at(m)))

    def qd_copy(m, whose):
        return remote(qd_out.at[at(m)], qd.at[chunk(whose), :], qd_s.at[m], qd_r.at[m], (seg, at(m)))

    def x_copy(m, whose):
        block = piece(whose, at(m))
        return remote(block, block, x_s.at[m], x_r.at[m], (across, lane))

    def c_copy(n, m, whose):
        block = piece(whose, at(m))
        return remote(block, block, c_s.at[n, m], c_r.at[n, m], (other, lane))

    def od_copy(m, whose):
        return remote(od.at[chunk(at(m)), :], od_in.at[whose, 0], od_s.at[m], od_r.at[m], (seg, at(m)))

    def send_kv(m):
        kv_copy(m, lane).start()

    def send_qd(m):
        qd_copy(m, lane).start()

    def forward(m):
        x_copy(m, across).wait_recv()
        c_copy(1, m, across).start()

    def to_near(m):
        x_copy(m, seg).start()
        c_copy(0, m, seg).start()

    def arrive(m):
        kv_copy(m, at(m)).wait_recv()
        to_near(m)

    loads[0].wait()
    loads[1].wait()
    pack(k_ref, v_ref, kv_out)
    pl.semaphore_wait(barrier, lanes + 1)
    for k in range(1, half):
        send_kv(lanes - k)
        send_kv(k)
    send_kv(half)
    kv[pl.ds(2 * (seg * lanes + lane), 2)] = kv_out[lane]
    to_near(0)
    loads[2].wait()
    loads[3].wait()
    pack(q_ref, g_ref, qd_out)
    qd[chunk(lane), :] = qd_out[lane]
    loads[4].wait()
    link_terms(lanes, seg, lane, lists_v, chain_v)
    chain_copy = pltpu.make_async_copy(chain_v, chain, idx_s.at[0])
    chain_copy.start()
    sums[LANES] = jnp.zeros((BLK, PAIR), jnp.float32)

    for m in range(1, half):
        arrive(m)
    for k in range(1, half + 1):
        arrive(lanes - k)
        send_qd(lanes - k)
        if k < half:
            send_qd(k)
        for m in ((0, 1), (2, 3), (7,), (6, 5, 4))[k - 1]:
            forward(m)

    def complete(m):
        c_copy(0, m, other).wait_recv()
        c_copy(1, m, beyond).wait_recv()

    loop(0, lanes, complete)
    loads[5].wait()
    loads[6].wait()
    chain_copy.wait()

    def score(n, slot):
        for i in range(2):
            score_block(qd, kv, lists, 2 * at(chunk_at(lanes, n)) + i, both.at[slot, i])

    def softmax(n, slot):
        for i in range(2):
            softmax_block(counts, 2 * at(chunk_at(lanes, n)) + i, both.at[slot, i], stacked.at[slot, i])

    def gradient(n, slot):
        for i in range(2):
            block = 2 * at(chunk_at(lanes, n)) + i
            gradient_block(qd, kv, lists, chain, block, (2 * n + i) * KSEL, stacked.at[slot, i], od, sums)

    def receive_qd(n):
        m = chunk_at(lanes, n)
        qd_copy(m, at(m)).wait_recv()

    def send_od(n):
        od_copy(chunk_at(lanes, n), lane).start()

    receive_qd(0)
    score(0, 0)
    softmax(0, 0)
    score(1, 1)

    def two_steps(n):
        receive_qd(n)
        gradient(n - 2, 0)
        softmax(n - 1, 1)
        score(n, 0)
        send_od(n - 2)
        receive_qd(n + 1)
        gradient(n - 1, 1)
        softmax(n, 0)
        score(n + 1, 1)

        @pl.when(n > 2)
        def _():
            send_od(n - 1)

    loop(1, half, lambda k: two_steps(2 * k))
    gradient(lanes - 2, 0)
    softmax(lanes - 1, 1)
    send_od(lanes - 2)
    gradient(lanes - 1, 1)
    send_od(lanes - 1)

    def partial(whose, m):
        block = 2 * (whose * lanes + at(m))
        return jnp.concatenate([sums[chain[1, block + i]] for i in range(2)], axis=0)

    def dc_copy(n, m):
        return remote(core_out.at[n, m], core_in.at[n, m], dc_s.at[n, m], dc_r.at[n, m], (other, lane))

    def dx_copy(m):
        return remote(x_out.at[m], x_in.at[m], dx_s.at[m], dx_r.at[m], (across, lane))

    def end_copy(m, whose):
        return remote(end_out.at[m], end_in.at[whose, 0], e_s.at[m], e_r.at[m], (seg, at(m)))

    def to_core(n, m, whose):
        core_out[n, m] = partial(whose, m).astype(jnp.bfloat16)
        dc_copy(n, m).start()

    def to_chip(m):
        dc_copy(1, m).wait_recv()
        x_out[m] = (partial(across, m) + core_in[1, m].astype(jnp.float32)).astype(jnp.bfloat16)
        dx_copy(m).start()
        to_core(0, m, other)

    def total(m):
        mine = partial(seg, m)
        dc_copy(0, m).wait_recv()
        dx_copy(m).wait_recv()
        near = core_in[0, m].astype(jnp.float32)
        return (mine + near + x_in[m].astype(jnp.float32)).astype(jnp.bfloat16)

    def to_owner(m):
        end_out[m] = total(m)
        end_copy(m, lane).start()

    loop(0, lanes, lambda i: to_core(1, lanes - 1 - i, beyond))
    loop(0, lanes, lambda i: to_chip(lanes - 1 - i))
    loop(0, lanes - 1, lambda i: to_owner(lanes - 1 - i))
    end_in[lane, 0] = total(0)
    od_in[lane, 0] = od[chunk(lane), :]

    def finish(m):
        for n in range(2):
            c_copy(n, m, seg).wait_send()
            dc_copy(n, m).wait_send()
        x_copy(m, seg).wait_send()
        dx_copy(m).wait_send()

    loop(0, lanes, finish)

    def finish_lanes(m):
        kv_copy(m, lane).wait_send()
        qd_copy(m, lane).wait_send()
        od_copy(m, lane).wait_send()
        od_copy(m, at(m)).wait_recv()
        end_copy(m, lane).wait_send()
        end_copy(m, at(m)).wait_recv()

    loop(1, lanes, finish_lanes)


def fits(lanes, heads_here, rows):
    return heads_here == 1 and rows == 2 * BLK and 2 * lanes * KSEL == LANES


def fused(lanes, query_rows, key_rows, value_rows, out_grad, block_lists, block_counts):
    rows, width = query_rows.shape
    segs, half, f32 = 4, jnp.bfloat16, jnp.float32
    vmem = pl.BlockSpec(memory_space=pltpu.VMEM)
    hbm = pl.BlockSpec(memory_space=pltpu.HBM)
    dma = pltpu.SemaphoreType.DMA
    lists = block_lists.T
    chunks = (lanes, rows, PAIR)
    buffers = (
        [((rows, width), half)] * 4
        + [(chunks, half), ((lanes, 2, BLK, PAIR), half)]
        + [((lanes * rows, PAIR), half), ((2 * segs * lanes, BLK, PAIR), half), ((lanes * rows, PAIR), half)]
        + [((LANES + 1, BLK, PAIR), f32)]
        + [((2, 2, 2 * BLK, KSEL * BLK), f32), ((2, 2, 2 * BLK, KSEL * BLK), half)]
        + [((2, *chunks), half)] * 2
        + [(chunks, half)] * 3
    )
    size = sum(math.prod(shape) * jnp.dtype(kind).itemsize for shape, kind in buffers)
    return pl.pallas_call(
        functools.partial(fused_kernel, lanes),
        out_shape=[jax.ShapeDtypeStruct((lanes, 1, rows, PAIR), half)] * 2,
        in_specs=[hbm] * 6,
        out_specs=[vmem] * 2,
        scratch_shapes=[pltpu.VMEM(*buffer) for buffer in buffers]
        + [pltpu.SMEM(lists.shape, jnp.int32), pltpu.SMEM(block_counts.shape, jnp.int32)]
        + [pltpu.VMEM(lists.shape, jnp.int32), pltpu.VMEM((8, LANES), jnp.int32), pltpu.SMEM((8, LANES), jnp.int32)]
        + [dma((7,)), dma((1,))]
        + [dma((lanes,))] * 6
        + [dma((2, lanes))] * 2
        + [dma((lanes,))] * 6
        + [dma((2, lanes))] * 2,
        compiler_params=pltpu.CompilerParams(
            collective_id=0, has_side_effects=True, vmem_limit_bytes=6 * MIB + size + 4 * lanes * rows * PAIR
        ),
        name="fused",
    )(
        *(
            pltpu.with_memory_space_constraint(a, pltpu.HBM)
            for a in (query_rows, key_rows, value_rows, out_grad, lists, block_counts)
        )
    )


def unpack_kernel(od, dkv, out_ref, dq_ref, dk_ref, dv_ref):
    for block, left, right in ((od, dq_ref, out_ref), (dkv, dk_ref, dv_ref)):
        heads_here = block.shape[1]
        for h in range(0, block.shape[0] * heads_here, 2):
            a, b = (block[g // heads_here, g % heads_here] for g in (h, h + 1))
            columns = slice(h * HDIM, (h + 2) * HDIM)
            left[:, columns] = join(a[:, :HDIM], b[:, :HDIM])
            right[:, columns] = join(a[:, HDIM:], b[:, HDIM:])


def comm_params(number, chunks, block):
    chunk_bytes = 2 * math.prod(block)
    return pltpu.CompilerParams(
        collective_id=number, has_side_effects=True, vmem_limit_bytes=4 * MIB + chunks * chunk_bytes
    )


def staged(lanes, query_rows, key_rows, value_rows, out_grad, block_lists, block_counts):
    rows, width = query_rows.shape
    heads_here = width // HDIM // lanes
    segs = 4
    block = (heads_here, rows, PAIR)
    vmem = pl.BlockSpec(memory_space=pltpu.VMEM)
    dma = pltpu.SemaphoreType.DMA
    half = jnp.bfloat16
    chunks = jax.ShapeDtypeStruct((lanes, *block), half)

    qd, kv = pl.pallas_call(
        functools.partial(gather_kernel, lanes),
        out_shape=(chunks, jax.ShapeDtypeStruct((segs, lanes, *block), half)),
        in_specs=[pl.BlockSpec(memory_space=pltpu.HBM)] * 4,
        out_specs=(vmem, vmem),
        scratch_shapes=[pltpu.VMEM((rows, width), half)] * 4
        + [pltpu.VMEM((lanes, *block), half)] * 2
        + [dma((4,))]
        + [dma((lanes,))] * 6
        + [dma((2, lanes))] * 2,
        compiler_params=comm_params(0, 10 * lanes, block),
        name="gather",
    )(*(pltpu.with_memory_space_constraint(a, pltpu.HBM) for a in (query_rows, key_rows, value_rows, out_grad)))

    qd = qd.transpose(1, 0, 2, 3).reshape(heads_here, lanes * rows, PAIR)
    kv = kv.transpose(2, 0, 1, 3, 4).reshape(heads_here, segs * lanes * rows, PAIR)
    od, dkv = attention(block_lists, block_counts, qd, kv)
    od = od.reshape(heads_here, lanes, rows, PAIR).transpose(1, 0, 2, 3)
    dkv = dkv.reshape(heads_here, segs, lanes, rows, PAIR).transpose(1, 2, 0, 3, 4)

    od, dkv = pl.pallas_call(
        functools.partial(return_kernel, lanes),
        out_shape=[chunks] * 2,
        in_specs=[vmem] * 2,
        out_specs=[vmem] * 2,
        scratch_shapes=[pltpu.VMEM((2, lanes, *block), half)]
        + [pltpu.VMEM((lanes, *block), half)] * 3
        + [dma((lanes + 1,))] * 2
        + [dma((2, lanes + 1))] * 2
        + [dma((lanes + 1,))] * 4,
        compiler_params=comm_params(1, 14 * lanes, block),
        name="scatter",
    )(od, dkv)

    return od, dkv


def on_device(lanes, *arrays):
    rows, width = arrays[0].shape
    half = jnp.bfloat16
    vmem = pl.BlockSpec(memory_space=pltpu.VMEM)
    gather = fused if fits(lanes, width // HDIM // lanes, rows) else staged
    od, dkv = gather(lanes, *arrays)
    return pl.pallas_call(
        unpack_kernel,
        out_shape=[jax.ShapeDtypeStruct((rows, width), half)] * 4,
        in_specs=[vmem] * 2,
        out_specs=[vmem] * 4,
        compiler_params=pltpu.CompilerParams(vmem_limit_bytes=4 * MIB + 32 * rows * width),
        name="unpack",
    )(od, dkv)


def solution(mesh):
    tokens = P(("blk", "uly"), None)
    return jax.shard_map(
        functools.partial(on_device, mesh.shape["uly"]),
        mesh=mesh,
        in_specs=(tokens, tokens, tokens, tokens, P("blk", None), P("blk")),
        out_specs=(tokens, tokens, tokens, tokens),
        check_vma=False,
    )
```

```python
import functools
import math

import jax
import jax.numpy as jnp
from jax import lax
from jax.experimental import pallas as pl
from jax.experimental.pallas import tpu as pltpu
from jax.sharding import PartitionSpec as P

HDIM = 64
BLK = 64
KSEL = 8
PAIR = 2 * HDIM
SCALE = 1.0 / math.sqrt(HDIM)
GROUP = 16
MIB = 1024 * 1024
LANES = 128


def dot(a, b, dims):
    return lax.dot_general(a, b, (dims, ((), ())), preferred_element_type=jnp.float32)


def attention_kernel(group, lists_hbm, counts_hbm, qd, kv, od, dkv, lists, counts, acc, sems):
    loads = (
        pltpu.make_async_copy(lists_hbm, lists, sems.at[0]),
        pltpu.make_async_copy(counts_hbm, counts, sems.at[1]),
    )
    for load in loads:
        load.start()
    for h in range(qd.shape[0]):
        acc[...] = jnp.zeros_like(acc)
        if h == 0:
            for load in loads:
                load.wait()
        attend_head(group, lists, counts, qd.at[h], kv.at[h], od.at[h], acc)
        dkv[h] = acc[...].astype(dkv.dtype)


def attend_head(group, lists, counts, qd_ref, kv_ref, od_ref, acc):
    local_blocks = qd_ref.shape[0] // BLK
    lane = lax.broadcasted_iota(jnp.int32, (BLK, PAIR), 1)
    first = lane < HDIM
    column = lax.broadcasted_iota(jnp.int32, (BLK, KSEL * BLK), 1)

    def one_block(b):
        rows = pl.ds(pl.multiple_of(b * BLK, BLK), BLK)
        picks = [pl.ds(pl.multiple_of(lists[j, b] * BLK, BLK), BLK) for j in range(KSEL)]
        qd = qd_ref[rows, :]
        zero = jnp.zeros_like(qd)
        diag = jnp.concatenate([jnp.where(first, qd * SCALE, zero), jnp.where(first, zero, qd)], axis=0)
        kv = jnp.concatenate([kv_ref[pick, :] for pick in picks], axis=0)
        both = dot(diag, kv, ((1,), (1,)))
        scores = jnp.where(column < counts[b] * BLK, both[:BLK], -1e30)
        weights = jnp.exp(scores - jnp.max(scores, axis=1, keepdims=True))
        prob = weights * (1.0 / jnp.sum(weights, axis=1, keepdims=True))
        rounded = prob.astype(jnp.bfloat16)
        delta = jnp.sum(rounded.astype(jnp.float32) * both[BLK:], axis=1, keepdims=True)
        grad_score = (prob * (both[BLK:] - delta)).astype(jnp.bfloat16)
        stacked = jnp.concatenate([grad_score, rounded], axis=0)
        rows_out = dot(stacked, kv, ((1,), (0,)))
        od_ref[rows, :] = jnp.where(first, rows_out[:BLK] * SCALE, rows_out[BLK:]).astype(jnp.bfloat16)
        terms = dot(stacked, diag, ((0,), (0,)))
        return picks, terms

    def turn(g, carry):
        done = [one_block(g * group + i) for i in range(group)]
        for picks, terms in done:
            for j, pick in enumerate(picks):
                acc[pick, :] += terms[j * BLK : (j + 1) * BLK]
        return carry

    lax.fori_loop(0, local_blocks // group, turn, 0)

def attention(block_lists, block_counts, qd, kv):
    heads_here, seg_rows, _ = qd.shape
    all_rows = kv.shape[1]
    vmem = pl.BlockSpec(memory_space=pltpu.VMEM)
    hbm = pl.BlockSpec(memory_space=pltpu.HBM)
    lists = block_lists.T
    limit = 6 * MIB + 4 * all_rows * PAIR + 4 * heads_here * (all_rows + seg_rows) * PAIR
    return pl.pallas_call(
        functools.partial(attention_kernel, math.gcd(GROUP, seg_rows // BLK)),
        out_shape=(
            jax.ShapeDtypeStruct(qd.shape, jnp.bfloat16),
            jax.ShapeDtypeStruct(kv.shape, jnp.bfloat16),
        ),
        in_specs=[hbm, hbm, vmem, vmem],
        out_specs=(vmem, vmem),
        scratch_shapes=[
            pltpu.SMEM(lists.shape, jnp.int32),
            pltpu.SMEM(block_counts.shape, jnp.int32),
            pltpu.VMEM((all_rows, PAIR), jnp.float32),
            pltpu.SemaphoreType.DMA((2,)),
        ],
        compiler_params=pltpu.CompilerParams(vmem_limit_bytes=limit),
        name="attention",
    )(
        pltpu.with_memory_space_constraint(lists, pltpu.HBM),
        pltpu.with_memory_space_constraint(block_counts, pltpu.HBM),
        qd,
        kv,
    )


MESH = pl.DeviceIdType.MESH


def places():
    seg, lane = lax.axis_index("blk"), lax.axis_index("uly")
    core = lax.rem(seg, 2)
    return seg, lane, seg + 1 - 2 * core, lax.rem(seg + 2, 4)


def remote(src, dst, send, recv, device):
    return pltpu.make_async_remote_copy(
        src_ref=src, dst_ref=dst, send_sem=send, recv_sem=recv, device_id=device, device_id_type=MESH
    )


def greet(lanes, diagonal=False):
    seg, lane, other, across = places()
    barrier = pltpu.get_barrier_semaphore()

    def one(i, carry):
        device = (seg, lax.rem(lane + i, lanes))
        pl.semaphore_signal(barrier, inc=1, device_id=device, device_id_type=MESH)
        return carry

    lax.fori_loop(1, lanes, one, 0)
    for near in (other, across, lax.rem(other + 2, 4))[: 3 if diagonal else 2]:
        pl.semaphore_signal(barrier, inc=1, device_id=(near, lane), device_id_type=MESH)
    return barrier


def loop(start, stop, body):
    lax.fori_loop(start, stop, lambda i, carry: (body(i), carry)[1], 0)


def join(left, right):
    return jnp.concatenate([left, right], axis=1)


def gather_kernel(
    lanes, q_hbm, k_hbm, v_hbm, g_hbm, qd, kv,
    k_ref, v_ref, q_ref, g_ref, qd_out, kv_out, in_s, qd_s, qd_r, kv_s, kv_r, x_s, x_r, c_s, c_r,
):
    pairs = ((k_hbm, k_ref), (v_hbm, v_ref), (q_hbm, q_ref), (g_hbm, g_ref))
    loads = [pltpu.make_async_copy(*pair, in_s.at[n]) for n, pair in enumerate(pairs)]
    for load in loads:
        load.start()
    seg, lane, other, across = places()
    heads_here = qd.shape[1]
    barrier = greet(lanes, True)

    def pack(left, right, to):
        for h in range(lanes * heads_here):
            columns = slice(h * HDIM, (h + 1) * HDIM)
            to[h // heads_here, h % heads_here] = join(left[:, columns], right[:, columns])

    loads[0].wait()
    loads[1].wait()
    pack(k_ref, v_ref, kv_out)
    pl.semaphore_wait(barrier, lanes + 2)

    def kv_copy(i, target, source):
        return remote(kv_out.at[target], kv.at[seg, source], kv_s.at[i], kv_r.at[i], (seg, target))

    def qd_copy(i, target, source):
        return remote(qd_out.at[target], qd.at[source], qd_s.at[i], qd_r.at[i], (seg, target))

    def x_copy(i, source, whose):
        return remote(kv.at[whose, source], kv.at[whose, source], x_s.at[i], x_r.at[i], (across, lane))

    def c_copy(n, i, source, whose):
        block = kv.at[whose, source]
        near = other if n == 0 else lax.rem(other + 2, 4)
        return remote(block, block, c_s.at[n, i], c_r.at[n, i], (near, lane))

    def ahead(i):
        return lax.rem(lane + i, lanes)

    def behind(i):
        return lax.rem(lane + lanes - i, lanes)

    loop(1, lanes, lambda i: kv_copy(i, ahead(i), lane).start())
    kv[seg, lane] = kv_out[lane]
    x_copy(0, lane, seg).start()
    c_copy(1, 0, lane, seg).start()
    c_copy(0, 0, lane, seg).start()
    loads[2].wait()
    loads[3].wait()
    pack(q_ref, g_ref, qd_out)
    qd[lane] = qd_out[lane]

    def arrive(i):
        kv_copy(i, lane, behind(i)).wait_recv()
        x_copy(i, behind(i), seg).start()
        qd_copy(i, ahead(i), lane).start()
        c_copy(1, i, behind(i), seg).start()
        c_copy(0, i, behind(i), seg).start()

    loop(1, lanes, arrive)
    loop(0, lanes, lambda i: x_copy(i, behind(i), across).wait_recv())

    def finish(i):
        c_copy(0, i, behind(i), other).wait_recv()
        c_copy(1, i, behind(i), lax.rem(other + 2, 4)).wait_recv()
        x_copy(i, behind(i), seg).wait_send()
        c_copy(0, i, behind(i), seg).wait_send()
        c_copy(1, i, behind(i), seg).wait_send()

    loop(0, lanes, finish)

    def finish_lanes(i):
        qd_copy(i, lane, behind(i)).wait_recv()
        qd_copy(i, ahead(i), lane).wait_send()
        kv_copy(i, ahead(i), lane).wait_send()

    loop(1, lanes, finish_lanes)


def return_kernel(
    lanes, od, dkv, od_in, end_in, core_in, x_out, x_in, end_out,
    od_s, od_r, c_s, c_r, x_s, x_r, e_s, e_r,
):
    seg, lane, other, across = places()
    heads_here = od.shape[1]
    barrier = greet(lanes)

    def ahead(i):
        return lax.rem(lane + i, lanes)

    def behind(i):
        return lax.rem(lane + lanes - i, lanes)

    def od_copy(i, target, source):
        return remote(od.at[target], od_in.at[source], od_s.at[i], od_r.at[i], (seg, target))

    def end_copy(i, target, source):
        return remote(end_out.at[target], end_in.at[source], e_s.at[i], e_r.at[i], (seg, target))

    def c_copy(n, i, whose):
        return remote(dkv.at[whose, ahead(i)], core_in.at[n, ahead(i)], c_s.at[n, i], c_r.at[n, i], (other, lane))

    def x_copy(i):
        return remote(x_out.at[ahead(i)], x_in.at[ahead(i)], x_s.at[i], x_r.at[i], (across, lane))

    def send(i):
        c_copy(1, i, lax.rem(other + 2, 4)).start()
        c_copy(0, i, other).start()

    def wide(block):
        return block.astype(jnp.float32)

    def reduce_core(i):
        c_copy(1, i, other).wait_recv()
        to = ahead(i)
        x_out[to] = (wide(dkv[across, to]) + wide(core_in[1, to])).astype(jnp.bfloat16)
        x_copy(i).start()

    def total(i):
        c_copy(0, i, other).wait_recv()
        x_copy(i).wait_recv()
        to = ahead(i)
        return (wide(dkv[seg, to]) + wide(core_in[0, to]) + wide(x_in[to])).astype(jnp.bfloat16)

    def reduce_chip(i):
        end_out[ahead(i)] = total(i)
        end_copy(i, ahead(i), lane).start()

    lag = min(4, lanes - 1)
    pl.semaphore_wait(barrier, lanes + 1)
    loop(1, lanes + 1, send)
    loop(1, lanes, lambda i: od_copy(i, ahead(i), lane).start())
    od_in[lane] = od[lane]
    loop(1, lag + 1, reduce_core)

    def both(i):
        reduce_core(i)
        reduce_chip(i - lag)

    loop(lag + 1, lanes + 1, both)
    loop(lanes + 1 - lag, lanes, reduce_chip)
    end_in[lane] = total(lanes)

    def finish(i):
        c_copy(0, i, other).wait_send()
        c_copy(1, i, other).wait_send()
        x_copy(i).wait_send()

    loop(1, lanes + 1, finish)

    def finish_lanes(i):
        od_copy(i, lane, behind(i)).wait_recv()
        end_copy(i, lane, behind(i)).wait_recv()
        od_copy(i, ahead(i), lane).wait_send()
        end_copy(i, ahead(i), lane).wait_send()

    loop(1, lanes, finish_lanes)


def exchange(lanes, lane, m):
    partner, bit = 0, 1
    while bit < lanes:
        partner += bit * lax.rem(lax.div(lane, bit) + m // bit, 2)
        bit *= 2
    return partner


def chunk_at(lanes, n):
    return lax.rem(n + 1, 2) * (lanes - 1 - n // 2) + lax.rem(n, 2) * (n // 2)


def block_diagonal(qd):
    first = lax.broadcasted_iota(jnp.int32, qd.shape, 1) < HDIM
    zero = jnp.zeros_like(qd)
    return jnp.concatenate([jnp.where(first, qd * SCALE, zero), jnp.where(first, zero, qd)], axis=0)


def block_rows(b):
    return pl.ds(pl.multiple_of(b * BLK, BLK), BLK)


def seen_rows(kv, lists, b):
    return jnp.concatenate([kv[lists[j, b]] for j in range(KSEL)], axis=0)


def score_block(qd, kv, lists, b, both):
    both[...] = dot(block_diagonal(qd[block_rows(b), :]), seen_rows(kv, lists, b), ((1,), (1,)))


def softmax_block(counts, b, both, stacked):
    column = lax.broadcasted_iota(jnp.int32, (1, KSEL * BLK), 1)
    scores = jnp.where(column < counts[b] * BLK, both[:BLK, :], -1e30)
    weights = jnp.exp(scores - jnp.max(scores, axis=1, keepdims=True))
    prob = weights * (1.0 / jnp.sum(weights, axis=1, keepdims=True))
    stacked[BLK:, :] = prob.astype(jnp.bfloat16)
    grad_prob = both[BLK:, :]
    delta = jnp.sum(prob * grad_prob, axis=1, keepdims=True)
    stacked[:BLK, :] = (prob * (grad_prob - delta)).astype(jnp.bfloat16)


def gradient_block(qd, kv, lists, chain, b, slot, stacked, od, sums):
    first = lax.broadcasted_iota(jnp.int32, (BLK, PAIR), 1) < HDIM
    both = stacked[...]
    rows_out = dot(both, seen_rows(kv, lists, b), ((1,), (0,)))
    od[block_rows(b), :] = jnp.where(first, rows_out[:BLK] * SCALE, rows_out[BLK:]).astype(jnp.bfloat16)
    terms = dot(both, block_diagonal(qd[block_rows(b), :]), ((0,), (0,)))
    for j in range(KSEL):
        before = sums[chain[0, j * (LANES // KSEL) + b]]
        sums[slot + j] = before + terms[j * BLK : (j + 1) * BLK]


def link_terms(lanes, seg, lane, lists, out):
    blocks = 2 * lanes

    def iota(shape, axis):
        return lax.broadcasted_iota(jnp.int32, shape, axis)

    def parts(axis):
        entry = iota((LANES, LANES), axis)
        j, b = lax.div(entry, blocks), lax.rem(entry, blocks)
        m = jnp.bitwise_xor(lax.div(b, 2), lane)
        turn = jnp.where(m < lanes // 2, 2 * m + 1, 2 * (lanes - 1 - m))
        return j, b, 2 * turn + lax.rem(b, 2)

    wide = jnp.concatenate([lists[...]] * (LANES // blocks), axis=1)
    own_row = iota((KSEL, LANES), 0) == lax.div(iota((KSEL, LANES), 1), blocks)
    row = jnp.sum(jnp.where(own_row, wide, 0), axis=0, keepdims=True)
    across = jnp.broadcast_to(row, (LANES, LANES))
    down = across.T
    j, b, when = parts(0)
    now = parts(1)[2]
    slot = KSEL * when + j
    valid = jnp.logical_or(j == 0, down != seg * blocks + b)
    earlier = jnp.logical_and(jnp.logical_and(down == across, when < now), valid)
    same = jnp.logical_and(down == iota((LANES, LANES), 1), valid)
    for n, chosen in enumerate((earlier, same)):
        latest = jnp.max(jnp.where(chosen, slot, -1), axis=0, keepdims=True)
        out[n : n + 1, :] = jnp.where(latest < 0, LANES, latest)


def fused_kernel(
    lanes, q_hbm, k_hbm, v_hbm, g_hbm, lists_hbm, counts_hbm, od_in, end_in,
    k_ref, v_ref, q_ref, g_ref, qd_out, kv_out, qd, kv, od, sums, both, stacked,
    core_out, core_in, x_out, x_in, end_out, lists, counts, lists_v, chain_v, chain,
    in_s, idx_s, kv_s, kv_r, qd_s, qd_r, x_s, x_r, c_s, c_r, od_s, od_r, e_s, e_r, dx_s, dx_r, dc_s, dc_r,
):
    rows = q_hbm.shape[0]
    half = lanes // 2
    pairs = (
        (k_hbm, k_ref), (v_hbm, v_ref), (q_hbm, q_ref), (g_hbm, g_ref),
        (lists_hbm, lists_v), (lists_hbm, lists), (counts_hbm, counts),
    )
    loads = [pltpu.make_async_copy(*pair, in_s.at[n]) for n, pair in enumerate(pairs)]
    for load in loads:
        load.start()
    seg, lane, other, across = places()
    beyond = lax.rem(other + 2, 4)
    barrier = greet(lanes)

    def at(m):
        return exchange(lanes, lane, m)

    def pack(left, right, to):
        for h in range(lanes):
            columns = slice(h * HDIM, (h + 1) * HDIM)
            to[h] = join(left[:, columns], right[:, columns]).reshape(to.shape[1:])

    def chunk(i):
        return pl.ds(pl.multiple_of(i * rows, rows), rows)

    def piece(whose, i):
        return kv.at[pl.ds(2 * (whose * lanes + i), 2)]

    def kv_copy(m, whose):
        return remote(kv_out.at[at(m)], piece(seg, whose), kv_s.at[m], kv_r.at[m], (seg, at(m)))

    def qd_copy(m, whose):
        return remote(qd_out.at[at(m)], qd.at[chunk(whose), :], qd_s.at[m], qd_r.at[m], (seg, at(m)))

    def x_copy(m, whose):
        block = piece(whose, at(m))
        return remote(block, block, x_s.at[m], x_r.at[m], (across, lane))

    def c_copy(n, m, whose):
        block = piece(whose, at(m))
        return remote(block, block, c_s.at[n, m], c_r.at[n, m], (other, lane))

    def od_copy(m, whose):
        return remote(od.at[chunk(at(m)), :], od_in.at[whose, 0], od_s.at[m], od_r.at[m], (seg, at(m)))

    def send_kv(m):
        kv_copy(m, lane).start()

    def send_qd(m):
        qd_copy(m, lane).start()

    def forward(m):
        x_copy(m, across).wait_recv()
        c_copy(1, m, across).start()

    def to_near(m):
        x_copy(m, seg).start()
        c_copy(0, m, seg).start()

    def arrive(m):
        kv_copy(m, at(m)).wait_recv()
        to_near(m)

    loads[0].wait()
    loads[1].wait()
    pack(k_ref, v_ref, kv_out)
    pl.semaphore_wait(barrier, lanes + 1)
    for k in range(1, half):
        send_kv(lanes - k)
        send_kv(k)
    send_kv(half)
    kv[pl.ds(2 * (seg * lanes + lane), 2)] = kv_out[lane]
    to_near(0)
    loads[2].wait()
    loads[3].wait()
    pack(q_ref, g_ref, qd_out)
    qd[chunk(lane), :] = qd_out[lane]
    loads[4].wait()
    link_terms(lanes, seg, lane, lists_v, chain_v)
    chain_copy = pltpu.make_async_copy(chain_v, chain, idx_s.at[0])
    chain_copy.start()
    sums[LANES] = jnp.zeros((BLK, PAIR), jnp.float32)

    for m in range(1, half):
        arrive(m)
    for k in range(1, half + 1):
        arrive(lanes - k)
        send_qd(lanes - k)
        if k < half:
            send_qd(k)
    for m in (0, 1, 2, 3, 7, 6, 5, 4):
        forward(m)

    def complete(m):
        c_copy(0, m, other).wait_recv()
        c_copy(1, m, beyond).wait_recv()

    loop(0, lanes, complete)
    loads[5].wait()
    loads[6].wait()
    chain_copy.wait()

    def score(n, slot):
        for i in range(2):
            score_block(qd, kv, lists, 2 * at(chunk_at(lanes, n)) + i, both.at[slot, i])

    def softmax(n, slot):
        for i in range(2):
            softmax_block(counts, 2 * at(chunk_at(lanes, n)) + i, both.at[slot, i], stacked.at[slot, i])

    def gradient(n, slot):
        for i in range(2):
            block = 2 * at(chunk_at(lanes, n)) + i
            gradient_block(qd, kv, lists, chain, block, (2 * n + i) * KSEL, stacked.at[slot, i], od, sums)

    def receive_qd(n):
        m = chunk_at(lanes, n)
        qd_copy(m, at(m)).wait_recv()

    def send_od(n):
        od_copy(chunk_at(lanes, n), lane).start()

    receive_qd(0)
    score(0, 0)
    softmax(0, 0)
    score(1, 1)

    def two_steps(n):
        receive_qd(n)
        gradient(n - 2, 0)
        softmax(n - 1, 1)
        score(n, 0)
        send_od(n - 2)
        receive_qd(n + 1)
        gradient(n - 1, 1)
        softmax(n, 0)
        score(n + 1, 1)

        @pl.when(n > 2)
        def _():
            send_od(n - 1)

    loop(1, half, lambda k: two_steps(2 * k))
    gradient(lanes - 2, 0)
    softmax(lanes - 1, 1)
    send_od(lanes - 2)
    gradient(lanes - 1, 1)
    send_od(lanes - 1)

    def partial(whose, m):
        block = 2 * (whose * lanes + at(m))
        return jnp.concatenate([sums[chain[1, block + i]] for i in range(2)], axis=0)

    def dc_copy(n, m):
        return remote(core_out.at[n, m], core_in.at[n, m], dc_s.at[n, m], dc_r.at[n, m], (other, lane))

    def dx_copy(m):
        return remote(x_out.at[m], x_in.at[m], dx_s.at[m], dx_r.at[m], (across, lane))

    def end_copy(m, whose):
        return remote(end_out.at[m], end_in.at[whose, 0], e_s.at[m], e_r.at[m], (seg, at(m)))

    def to_core(n, m, whose):
        core_out[n, m] = partial(whose, m).astype(jnp.bfloat16)
        dc_copy(n, m).start()

    def to_chip(m):
        dc_copy(1, m).wait_recv()
        x_out[m] = (partial(across, m) + core_in[1, m].astype(jnp.float32)).astype(jnp.bfloat16)
        dx_copy(m).start()
        to_core(0, m, other)

    def total(m):
        mine = partial(seg, m)
        dc_copy(0, m).wait_recv()
        dx_copy(m).wait_recv()
        near = core_in[0, m].astype(jnp.float32)
        return (mine + near + x_in[m].astype(jnp.float32)).astype(jnp.bfloat16)

    def to_owner(m):
        end_out[m] = total(m)
        end_copy(m, lane).start()

    loop(0, lanes, lambda i: to_core(1, lanes - 1 - i, beyond))
    loop(0, lanes, lambda i: to_chip(lanes - 1 - i))
    loop(0, lanes - 1, lambda i: to_owner(lanes - 1 - i))
    end_in[lane, 0] = total(0)
    od_in[lane, 0] = od[chunk(lane), :]

    def finish(m):
        for n in range(2):
            c_copy(n, m, seg).wait_send()
            dc_copy(n, m).wait_send()
        x_copy(m, seg).wait_send()
        dx_copy(m).wait_send()

    loop(0, lanes, finish)

    def finish_lanes(m):
        kv_copy(m, lane).wait_send()
        qd_copy(m, lane).wait_send()
        od_copy(m, lane).wait_send()
        od_copy(m, at(m)).wait_recv()
        end_copy(m, lane).wait_send()
        end_copy(m, at(m)).wait_recv()

    loop(1, lanes, finish_lanes)


def fits(lanes, heads_here, rows):
    return heads_here == 1 and rows == 2 * BLK and 2 * lanes * KSEL == LANES


def fused(lanes, query_rows, key_rows, value_rows, out_grad, block_lists, block_counts):
    rows, width = query_rows.shape
    segs, half, f32 = 4, jnp.bfloat16, jnp.float32
    vmem = pl.BlockSpec(memory_space=pltpu.VMEM)
    hbm = pl.BlockSpec(memory_space=pltpu.HBM)
    dma = pltpu.SemaphoreType.DMA
    lists = block_lists.T
    chunks = (lanes, rows, PAIR)
    buffers = (
        [((rows, width), half)] * 4
        + [(chunks, half), ((lanes, 2, BLK, PAIR), half)]
        + [((lanes * rows, PAIR), half), ((2 * segs * lanes, BLK, PAIR), half), ((lanes * rows, PAIR), half)]
        + [((LANES + 1, BLK, PAIR), f32)]
        + [((2, 2, 2 * BLK, KSEL * BLK), f32), ((2, 2, 2 * BLK, KSEL * BLK), half)]
        + [((2, *chunks), half)] * 2
        + [(chunks, half)] * 3
    )
    size = sum(math.prod(shape) * jnp.dtype(kind).itemsize for shape, kind in buffers)
    return pl.pallas_call(
        functools.partial(fused_kernel, lanes),
        out_shape=[jax.ShapeDtypeStruct((lanes, 1, rows, PAIR), half)] * 2,
        in_specs=[hbm] * 6,
        out_specs=[vmem] * 2,
        scratch_shapes=[pltpu.VMEM(*buffer) for buffer in buffers]
        + [pltpu.SMEM(lists.shape, jnp.int32), pltpu.SMEM(block_counts.shape, jnp.int32)]
        + [pltpu.VMEM(lists.shape, jnp.int32), pltpu.VMEM((8, LANES), jnp.int32), pltpu.SMEM((8, LANES), jnp.int32)]
        + [dma((7,)), dma((1,))]
        + [dma((lanes,))] * 6
        + [dma((2, lanes))] * 2
        + [dma((lanes,))] * 6
        + [dma((2, lanes))] * 2,
        compiler_params=pltpu.CompilerParams(
            collective_id=0, has_side_effects=True, vmem_limit_bytes=6 * MIB + size + 4 * lanes * rows * PAIR
        ),
        name="fused",
    )(
        *(
            pltpu.with_memory_space_constraint(a, pltpu.HBM)
            for a in (query_rows, key_rows, value_rows, out_grad, lists, block_counts)
        )
    )


def unpack_kernel(od, dkv, out_ref, dq_ref, dk_ref, dv_ref):
    for block, left, right in ((od, dq_ref, out_ref), (dkv, dk_ref, dv_ref)):
        heads_here = block.shape[1]
        for h in range(0, block.shape[0] * heads_here, 2):
            a, b = (block[g // heads_here, g % heads_here] for g in (h, h + 1))
            columns = slice(h * HDIM, (h + 2) * HDIM)
            left[:, columns] = join(a[:, :HDIM], b[:, :HDIM])
            right[:, columns] = join(a[:, HDIM:], b[:, HDIM:])


def comm_params(number, chunks, block):
    chunk_bytes = 2 * math.prod(block)
    return pltpu.CompilerParams(
        collective_id=number, has_side_effects=True, vmem_limit_bytes=4 * MIB + chunks * chunk_bytes
    )


def staged(lanes, query_rows, key_rows, value_rows, out_grad, block_lists, block_counts):
    rows, width = query_rows.shape
    heads_here = width // HDIM // lanes
    segs = 4
    block = (heads_here, rows, PAIR)
    vmem = pl.BlockSpec(memory_space=pltpu.VMEM)
    dma = pltpu.SemaphoreType.DMA
    half = jnp.bfloat16
    chunks = jax.ShapeDtypeStruct((lanes, *block), half)

    qd, kv = pl.pallas_call(
        functools.partial(gather_kernel, lanes),
        out_shape=(chunks, jax.ShapeDtypeStruct((segs, lanes, *block), half)),
        in_specs=[pl.BlockSpec(memory_space=pltpu.HBM)] * 4,
        out_specs=(vmem, vmem),
        scratch_shapes=[pltpu.VMEM((rows, width), half)] * 4
        + [pltpu.VMEM((lanes, *block), half)] * 2
        + [dma((4,))]
        + [dma((lanes,))] * 6
        + [dma((2, lanes))] * 2,
        compiler_params=comm_params(0, 10 * lanes, block),
        name="gather",
    )(*(pltpu.with_memory_space_constraint(a, pltpu.HBM) for a in (query_rows, key_rows, value_rows, out_grad)))

    qd = qd.transpose(1, 0, 2, 3).reshape(heads_here, lanes * rows, PAIR)
    kv = kv.transpose(2, 0, 1, 3, 4).reshape(heads_here, segs * lanes * rows, PAIR)
    od, dkv = attention(block_lists, block_counts, qd, kv)
    od = od.reshape(heads_here, lanes, rows, PAIR).transpose(1, 0, 2, 3)
    dkv = dkv.reshape(heads_here, segs, lanes, rows, PAIR).transpose(1, 2, 0, 3, 4)

    od, dkv = pl.pallas_call(
        functools.partial(return_kernel, lanes),
        out_shape=[chunks] * 2,
        in_specs=[vmem] * 2,
        out_specs=[vmem] * 2,
        scratch_shapes=[pltpu.VMEM((2, lanes, *block), half)]
        + [pltpu.VMEM((lanes, *block), half)] * 3
        + [dma((lanes + 1,))] * 2
        + [dma((2, lanes + 1))] * 2
        + [dma((lanes + 1,))] * 4,
        compiler_params=comm_params(1, 14 * lanes, block),
        name="scatter",
    )(od, dkv)

    return od, dkv


def on_device(lanes, *arrays):
    rows, width = arrays[0].shape
    half = jnp.bfloat16
    vmem = pl.BlockSpec(memory_space=pltpu.VMEM)
    gather = fused if fits(lanes, width // HDIM // lanes, rows) else staged
    od, dkv = gather(lanes, *arrays)
    return pl.pallas_call(
        unpack_kernel,
        out_shape=[jax.ShapeDtypeStruct((rows, width), half)] * 4,
        in_specs=[vmem] * 2,
        out_specs=[vmem] * 4,
        compiler_params=pltpu.CompilerParams(vmem_limit_bytes=4 * MIB + 32 * rows * width),
        name="unpack",
    )(od, dkv)


def solution(mesh):
    tokens = P(("blk", "uly"), None)
    return jax.shard_map(
        functools.partial(on_device, mesh.shape["uly"]),
        mesh=mesh,
        in_specs=(tokens, tokens, tokens, tokens, P("blk", None), P("blk")),
        out_specs=(tokens, tokens, tokens, tokens),
        check_vma=False,
    )
```

```python
import functools
import math

import jax
import jax.numpy as jnp
from jax import lax
from jax.experimental import pallas as pl
from jax.experimental.pallas import tpu as pltpu
from jax.sharding import PartitionSpec as P

HDIM = 64
BLK = 64
KSEL = 8
PAIR = 2 * HDIM
SCALE = 1.0 / math.sqrt(HDIM)
GROUP = 16
MIB = 1024 * 1024
LANES = 128


def dot(a, b, dims):
    return lax.dot_general(a, b, (dims, ((), ())), preferred_element_type=jnp.float32)


def attention_kernel(group, lists_hbm, counts_hbm, qd, kv, od, dkv, lists, counts, acc, sems):
    loads = (
        pltpu.make_async_copy(lists_hbm, lists, sems.at[0]),
        pltpu.make_async_copy(counts_hbm, counts, sems.at[1]),
    )
    for load in loads:
        load.start()
    for h in range(qd.shape[0]):
        acc[...] = jnp.zeros_like(acc)
        if h == 0:
            for load in loads:
                load.wait()
        attend_head(group, lists, counts, qd.at[h], kv.at[h], od.at[h], acc)
        dkv[h] = acc[...].astype(dkv.dtype)


def attend_head(group, lists, counts, qd_ref, kv_ref, od_ref, acc):
    local_blocks = qd_ref.shape[0] // BLK
    lane = lax.broadcasted_iota(jnp.int32, (BLK, PAIR), 1)
    first = lane < HDIM
    column = lax.broadcasted_iota(jnp.int32, (BLK, KSEL * BLK), 1)

    def one_block(b):
        rows = pl.ds(pl.multiple_of(b * BLK, BLK), BLK)
        picks = [pl.ds(pl.multiple_of(lists[j, b] * BLK, BLK), BLK) for j in range(KSEL)]
        qd = qd_ref[rows, :]
        zero = jnp.zeros_like(qd)
        diag = jnp.concatenate([jnp.where(first, qd * SCALE, zero), jnp.where(first, zero, qd)], axis=0)
        kv = jnp.concatenate([kv_ref[pick, :] for pick in picks], axis=0)
        both = dot(diag, kv, ((1,), (1,)))
        scores = jnp.where(column < counts[b] * BLK, both[:BLK], -1e30)
        weights = jnp.exp(scores - jnp.max(scores, axis=1, keepdims=True))
        prob = weights * (1.0 / jnp.sum(weights, axis=1, keepdims=True))
        rounded = prob.astype(jnp.bfloat16)
        delta = jnp.sum(rounded.astype(jnp.float32) * both[BLK:], axis=1, keepdims=True)
        grad_score = (prob * (both[BLK:] - delta)).astype(jnp.bfloat16)
        stacked = jnp.concatenate([grad_score, rounded], axis=0)
        rows_out = dot(stacked, kv, ((1,), (0,)))
        od_ref[rows, :] = jnp.where(first, rows_out[:BLK] * SCALE, rows_out[BLK:]).astype(jnp.bfloat16)
        terms = dot(stacked, diag, ((0,), (0,)))
        return picks, terms

    def turn(g, carry):
        done = [one_block(g * group + i) for i in range(group)]
        for picks, terms in done:
            for j, pick in enumerate(picks):
                acc[pick, :] += terms[j * BLK : (j + 1) * BLK]
        return carry

    lax.fori_loop(0, local_blocks // group, turn, 0)

def attention(block_lists, block_counts, qd, kv):
    heads_here, seg_rows, _ = qd.shape
    all_rows = kv.shape[1]
    vmem = pl.BlockSpec(memory_space=pltpu.VMEM)
    hbm = pl.BlockSpec(memory_space=pltpu.HBM)
    lists = block_lists.T
    limit = 6 * MIB + 4 * all_rows * PAIR + 4 * heads_here * (all_rows + seg_rows) * PAIR
    return pl.pallas_call(
        functools.partial(attention_kernel, math.gcd(GROUP, seg_rows // BLK)),
        out_shape=(
            jax.ShapeDtypeStruct(qd.shape, jnp.bfloat16),
            jax.ShapeDtypeStruct(kv.shape, jnp.bfloat16),
        ),
        in_specs=[hbm, hbm, vmem, vmem],
        out_specs=(vmem, vmem),
        scratch_shapes=[
            pltpu.SMEM(lists.shape, jnp.int32),
            pltpu.SMEM(block_counts.shape, jnp.int32),
            pltpu.VMEM((all_rows, PAIR), jnp.float32),
            pltpu.SemaphoreType.DMA((2,)),
        ],
        compiler_params=pltpu.CompilerParams(vmem_limit_bytes=limit),
        name="attention",
    )(
        pltpu.with_memory_space_constraint(lists, pltpu.HBM),
        pltpu.with_memory_space_constraint(block_counts, pltpu.HBM),
        qd,
        kv,
    )


MESH = pl.DeviceIdType.MESH


def places():
    seg, lane = lax.axis_index("blk"), lax.axis_index("uly")
    core = lax.rem(seg, 2)
    return seg, lane, seg + 1 - 2 * core, lax.rem(seg + 2, 4)


def remote(src, dst, send, recv, device):
    return pltpu.make_async_remote_copy(
        src_ref=src, dst_ref=dst, send_sem=send, recv_sem=recv, device_id=device, device_id_type=MESH
    )


def greet(lanes, diagonal=False):
    seg, lane, other, across = places()
    barrier = pltpu.get_barrier_semaphore()

    def one(i, carry):
        device = (seg, lax.rem(lane + i, lanes))
        pl.semaphore_signal(barrier, inc=1, device_id=device, device_id_type=MESH)
        return carry

    lax.fori_loop(1, lanes, one, 0)
    for near in (other, across, lax.rem(other + 2, 4))[: 3 if diagonal else 2]:
        pl.semaphore_signal(barrier, inc=1, device_id=(near, lane), device_id_type=MESH)
    return barrier


def loop(start, stop, body):
    lax.fori_loop(start, stop, lambda i, carry: (body(i), carry)[1], 0)


def join(left, right):
    return jnp.concatenate([left, right], axis=1)


def gather_kernel(
    lanes, q_hbm, k_hbm, v_hbm, g_hbm, qd, kv,
    k_ref, v_ref, q_ref, g_ref, qd_out, kv_out, in_s, qd_s, qd_r, kv_s, kv_r, x_s, x_r, c_s, c_r,
):
    pairs = ((k_hbm, k_ref), (v_hbm, v_ref), (q_hbm, q_ref), (g_hbm, g_ref))
    loads = [pltpu.make_async_copy(*pair, in_s.at[n]) for n, pair in enumerate(pairs)]
    for load in loads:
        load.start()
    seg, lane, other, across = places()
    heads_here = qd.shape[1]
    barrier = greet(lanes, True)

    def pack(left, right, to):
        for h in range(lanes * heads_here):
            columns = slice(h * HDIM, (h + 1) * HDIM)
            to[h // heads_here, h % heads_here] = join(left[:, columns], right[:, columns])

    loads[0].wait()
    loads[1].wait()
    pack(k_ref, v_ref, kv_out)
    pl.semaphore_wait(barrier, lanes + 2)

    def kv_copy(i, target, source):
        return remote(kv_out.at[target], kv.at[seg, source], kv_s.at[i], kv_r.at[i], (seg, target))

    def qd_copy(i, target, source):
        return remote(qd_out.at[target], qd.at[source], qd_s.at[i], qd_r.at[i], (seg, target))

    def x_copy(i, source, whose):
        return remote(kv.at[whose, source], kv.at[whose, source], x_s.at[i], x_r.at[i], (across, lane))

    def c_copy(n, i, source, whose):
        block = kv.at[whose, source]
        near = other if n == 0 else lax.rem(other + 2, 4)
        return remote(block, block, c_s.at[n, i], c_r.at[n, i], (near, lane))

    def ahead(i):
        return lax.rem(lane + i, lanes)

    def behind(i):
        return lax.rem(lane + lanes - i, lanes)

    loop(1, lanes, lambda i: kv_copy(i, ahead(i), lane).start())
    kv[seg, lane] = kv_out[lane]
    x_copy(0, lane, seg).start()
    c_copy(1, 0, lane, seg).start()
    c_copy(0, 0, lane, seg).start()
    loads[2].wait()
    loads[3].wait()
    pack(q_ref, g_ref, qd_out)
    qd[lane] = qd_out[lane]

    def arrive(i):
        kv_copy(i, lane, behind(i)).wait_recv()
        x_copy(i, behind(i), seg).start()
        qd_copy(i, ahead(i), lane).start()
        c_copy(1, i, behind(i), seg).start()
        c_copy(0, i, behind(i), seg).start()

    loop(1, lanes, arrive)
    loop(0, lanes, lambda i: x_copy(i, behind(i), across).wait_recv())

    def finish(i):
        c_copy(0, i, behind(i), other).wait_recv()
        c_copy(1, i, behind(i), lax.rem(other + 2, 4)).wait_recv()
        x_copy(i, behind(i), seg).wait_send()
        c_copy(0, i, behind(i), seg).wait_send()
        c_copy(1, i, behind(i), seg).wait_send()

    loop(0, lanes, finish)

    def finish_lanes(i):
        qd_copy(i, lane, behind(i)).wait_recv()
        qd_copy(i, ahead(i), lane).wait_send()
        kv_copy(i, ahead(i), lane).wait_send()

    loop(1, lanes, finish_lanes)


def return_kernel(
    lanes, od, dkv, od_in, end_in, core_in, x_out, x_in, end_out,
    od_s, od_r, c_s, c_r, x_s, x_r, e_s, e_r,
):
    seg, lane, other, across = places()
    heads_here = od.shape[1]
    barrier = greet(lanes)

    def ahead(i):
        return lax.rem(lane + i, lanes)

    def behind(i):
        return lax.rem(lane + lanes - i, lanes)

    def od_copy(i, target, source):
        return remote(od.at[target], od_in.at[source], od_s.at[i], od_r.at[i], (seg, target))

    def end_copy(i, target, source):
        return remote(end_out.at[target], end_in.at[source], e_s.at[i], e_r.at[i], (seg, target))

    def c_copy(n, i, whose):
        return remote(dkv.at[whose, ahead(i)], core_in.at[n, ahead(i)], c_s.at[n, i], c_r.at[n, i], (other, lane))

    def x_copy(i):
        return remote(x_out.at[ahead(i)], x_in.at[ahead(i)], x_s.at[i], x_r.at[i], (across, lane))

    def send(i):
        c_copy(1, i, lax.rem(other + 2, 4)).start()
        c_copy(0, i, other).start()

    def wide(block):
        return block.astype(jnp.float32)

    def reduce_core(i):
        c_copy(1, i, other).wait_recv()
        to = ahead(i)
        x_out[to] = (wide(dkv[across, to]) + wide(core_in[1, to])).astype(jnp.bfloat16)
        x_copy(i).start()

    def total(i):
        c_copy(0, i, other).wait_recv()
        x_copy(i).wait_recv()
        to = ahead(i)
        return (wide(dkv[seg, to]) + wide(core_in[0, to]) + wide(x_in[to])).astype(jnp.bfloat16)

    def reduce_chip(i):
        end_out[ahead(i)] = total(i)
        end_copy(i, ahead(i), lane).start()

    lag = min(4, lanes - 1)
    pl.semaphore_wait(barrier, lanes + 1)
    loop(1, lanes + 1, send)
    loop(1, lanes, lambda i: od_copy(i, ahead(i), lane).start())
    od_in[lane] = od[lane]
    loop(1, lag + 1, reduce_core)

    def both(i):
        reduce_core(i)
        reduce_chip(i - lag)

    loop(lag + 1, lanes + 1, both)
    loop(lanes + 1 - lag, lanes, reduce_chip)
    end_in[lane] = total(lanes)

    def finish(i):
        c_copy(0, i, other).wait_send()
        c_copy(1, i, other).wait_send()
        x_copy(i).wait_send()

    loop(1, lanes + 1, finish)

    def finish_lanes(i):
        od_copy(i, lane, behind(i)).wait_recv()
        end_copy(i, lane, behind(i)).wait_recv()
        od_copy(i, ahead(i), lane).wait_send()
        end_copy(i, ahead(i), lane).wait_send()

    loop(1, lanes, finish_lanes)


def exchange(lanes, lane, m):
    partner, bit = 0, 1
    while bit < lanes:
        partner += bit * lax.rem(lax.div(lane, bit) + m // bit, 2)
        bit *= 2
    return partner


def chunk_at(lanes, n):
    return lax.rem(n, 2) * (lanes - 1 - n // 2) + lax.rem(n + 1, 2) * (n // 2)


def block_diagonal(qd):
    first = lax.broadcasted_iota(jnp.int32, qd.shape, 1) < HDIM
    zero = jnp.zeros_like(qd)
    return jnp.concatenate([jnp.where(first, qd * SCALE, zero), jnp.where(first, zero, qd)], axis=0)


def block_rows(b):
    return pl.ds(pl.multiple_of(b * BLK, BLK), BLK)


def seen_rows(kv, lists, b):
    return jnp.concatenate([kv[lists[j, b]] for j in range(KSEL)], axis=0)


def score_block(qd, kv, lists, b, both):
    both[...] = dot(block_diagonal(qd[block_rows(b), :]), seen_rows(kv, lists, b), ((1,), (1,)))


def softmax_block(counts, b, both, stacked):
    column = lax.broadcasted_iota(jnp.int32, (1, KSEL * BLK), 1)
    scores = jnp.where(column < counts[b] * BLK, both[:BLK, :], -1e30)
    weights = jnp.exp(scores - jnp.max(scores, axis=1, keepdims=True))
    prob = weights * (1.0 / jnp.sum(weights, axis=1, keepdims=True))
    stacked[BLK:, :] = prob.astype(jnp.bfloat16)
    grad_prob = both[BLK:, :]
    delta = jnp.sum(prob * grad_prob, axis=1, keepdims=True)
    stacked[:BLK, :] = (prob * (grad_prob - delta)).astype(jnp.bfloat16)


def gradient_block(qd, kv, lists, chain, b, slot, stacked, od, sums):
    first = lax.broadcasted_iota(jnp.int32, (BLK, PAIR), 1) < HDIM
    both = stacked[...]
    rows_out = dot(both, seen_rows(kv, lists, b), ((1,), (0,)))
    od[block_rows(b), :] = jnp.where(first, rows_out[:BLK] * SCALE, rows_out[BLK:]).astype(jnp.bfloat16)
    terms = dot(both, block_diagonal(qd[block_rows(b), :]), ((0,), (0,)))
    for j in range(KSEL):
        before = sums[chain[0, j * (LANES // KSEL) + b]]
        sums[slot + j] = before + terms[j * BLK : (j + 1) * BLK]


def link_terms(lanes, seg, lane, lists, out):
    blocks = 2 * lanes

    def iota(shape, axis):
        return lax.broadcasted_iota(jnp.int32, shape, axis)

    def parts(axis):
        entry = iota((LANES, LANES), axis)
        j, b = lax.div(entry, blocks), lax.rem(entry, blocks)
        m = jnp.bitwise_xor(lax.div(b, 2), lane)
        turn = jnp.where(m < lanes // 2, 2 * m, 2 * (lanes - 1 - m) + 1)
        return j, b, 2 * turn + lax.rem(b, 2)

    wide = jnp.concatenate([lists[...]] * (LANES // blocks), axis=1)
    own_row = iota((KSEL, LANES), 0) == lax.div(iota((KSEL, LANES), 1), blocks)
    row = jnp.sum(jnp.where(own_row, wide, 0), axis=0, keepdims=True)
    across = jnp.broadcast_to(row, (LANES, LANES))
    down = across.T
    j, b, when = parts(0)
    now = parts(1)[2]
    slot = KSEL * when + j
    valid = jnp.logical_or(j == 0, down != seg * blocks + b)
    earlier = jnp.logical_and(jnp.logical_and(down == across, when < now), valid)
    same = jnp.logical_and(down == iota((LANES, LANES), 1), valid)
    for n, chosen in enumerate((earlier, same)):
        latest = jnp.max(jnp.where(chosen, slot, -1), axis=0, keepdims=True)
        out[n : n + 1, :] = jnp.where(latest < 0, LANES, latest)


def fused_kernel(
    lanes, q_hbm, k_hbm, v_hbm, g_hbm, lists_hbm, counts_hbm, out_ref, dq_ref, end_in,
    k_ref, v_ref, q_ref, g_ref, qd_out, kv_out, qd, kv, od, od_in, sums, both, stacked,
    core_out, core_in, x_out, x_in, end_out, lists, counts, lists_v, chain_v, chain,
    in_s, idx_s, kv_s, kv_r, qd_s, qd_r, x_s, x_r, c_s, c_r, od_s, od_r, e_s, e_r, dx_s, dx_r, dc_s, dc_r,
):
    rows = q_hbm.shape[0]
    half = lanes // 2
    pairs = (
        (k_hbm, k_ref), (v_hbm, v_ref), (q_hbm, q_ref), (g_hbm, g_ref),
        (lists_hbm, lists_v), (lists_hbm, lists), (counts_hbm, counts),
    )
    loads = [pltpu.make_async_copy(*pair, in_s.at[n]) for n, pair in enumerate(pairs)]
    seg, lane, other, across = places()
    beyond = lax.rem(other + 2, 4)
    partners = [exchange(lanes, lane, m) for m in range(lanes)]
    barrier = pltpu.get_barrier_semaphore()
    for device in [(seg, partners[m]) for m in range(lanes - 1, 0, -1)] + [(across, lane), (other, lane)]:
        pl.semaphore_signal(barrier, inc=1, device_id=device, device_id_type=MESH)
    for load in loads:
        load.start()

    def at(m):
        return partners[m] if isinstance(m, int) else exchange(lanes, lane, m)

    def each(order, body):
        for m in order:
            body(m)

    def pack(left, right, to):
        for h in range(lanes):
            columns = slice(h * HDIM, (h + 1) * HDIM)
            to[h] = join(left[:, columns], right[:, columns]).reshape(to.shape[1:])

    def chunk(i):
        return pl.ds(pl.multiple_of(i * rows, rows), rows)

    def piece(whose, i):
        return kv.at[pl.ds(2 * (whose * lanes + i), 2)]

    def kv_copy(m, whose):
        return remote(kv_out.at[at(m)], piece(seg, whose), kv_s.at[m], kv_r.at[m], (seg, at(m)))

    def qd_copy(m, whose):
        return remote(qd_out.at[at(m)], qd.at[chunk(whose), :], qd_s.at[m], qd_r.at[m], (seg, at(m)))

    def x_copy(m, whose):
        block = piece(whose, at(m))
        return remote(block, block, x_s.at[m], x_r.at[m], (across, lane))

    def c_copy(n, m, whose):
        block = piece(whose, at(m))
        return remote(block, block, c_s.at[n, m], c_r.at[n, m], (other, lane))

    def od_copy(m, whose):
        return remote(od.at[chunk(at(m)), :], od_in.at[whose], od_s.at[m], od_r.at[m], (seg, at(m)))

    def send_kv(m):
        kv_copy(m, lane).start()

    def send_qd(m):
        qd_copy(m, lane).start()

    def forward(m):
        x_copy(m, across).wait_recv()
        c_copy(1, m, across).start()

    def to_near(m):
        x_copy(m, seg).start()
        c_copy(0, m, seg).start()

    def arrive(m):
        kv_copy(m, at(m)).wait_recv()
        to_near(m)

    loads[0].wait()
    loads[1].wait()
    pack(k_ref, v_ref, kv_out)
    pl.semaphore_wait(barrier, lanes + 1)
    for k in range(1, half):
        send_kv(lanes - k)
        send_kv(k)
    send_kv(half)
    kv[pl.ds(2 * (seg * lanes + lane), 2)] = kv_out[lane]
    to_near(0)
    loads[2].wait()
    loads[3].wait()
    pack(q_ref, g_ref, qd_out)
    qd[chunk(lane), :] = qd_out[lane]
    loads[4].wait()
    link_terms(lanes, seg, lane, lists_v, chain_v)
    chain_copy = pltpu.make_async_copy(chain_v, chain, idx_s.at[0])
    chain_copy.start()
    sums[LANES] = jnp.zeros((BLK, PAIR), jnp.float32)

    near_first = list(range(1, half)) + list(range(lanes - 1, half - 1, -1))
    far_first = list(range(lanes - 1, -1, -1))
    each(near_first, arrive)
    for m in far_first[:half]:
        send_qd(m)
        if m > half:
            send_qd(lanes - m)
    each([0] + near_first, forward)

    def complete(m):
        c_copy(0, m, other).wait_recv()
        c_copy(1, m, beyond).wait_recv()

    each(far_first, complete)
    loads[5].wait()
    loads[6].wait()
    chain_copy.wait()

    def score(n, slot):
        for i in range(2):
            score_block(qd, kv, lists, 2 * at(chunk_at(lanes, n)) + i, both.at[slot, i])

    def softmax(n, slot):
        for i in range(2):
            softmax_block(counts, 2 * at(chunk_at(lanes, n)) + i, both.at[slot, i], stacked.at[slot, i])

    def gradient(n, slot):
        for i in range(2):
            block = 2 * at(chunk_at(lanes, n)) + i
            gradient_block(qd, kv, lists, chain, block, (2 * n + i) * KSEL, stacked.at[slot, i], od, sums)

    def receive_qd(n):
        m = chunk_at(lanes, n)
        qd_copy(m, at(m)).wait_recv()

    def send_od(n):
        od_copy(chunk_at(lanes, n), lane).start()

    score(0, 0)
    receive_qd(1)
    softmax(0, 0)
    score(1, 1)

    def two_steps(n):
        receive_qd(n)
        gradient(n - 2, 0)
        softmax(n - 1, 1)
        score(n, 0)

        @pl.when(n > 2)
        def _():
            send_od(n - 2)

        receive_qd(n + 1)
        gradient(n - 1, 1)
        softmax(n, 0)
        score(n + 1, 1)
        send_od(n - 1)

    loop(1, half, lambda k: two_steps(2 * k))
    gradient(lanes - 2, 0)
    softmax(lanes - 1, 1)
    send_od(lanes - 2)
    gradient(lanes - 1, 1)
    send_od(lanes - 1)

    def partial(whose, m):
        block = 2 * (whose * lanes + at(m))
        return jnp.concatenate([sums[chain[1, block + i]] for i in range(2)], axis=0)

    def dc_copy(n, m):
        return remote(core_out.at[n, m], core_in.at[n, m], dc_s.at[n, m], dc_r.at[n, m], (other, lane))

    def dx_copy(m):
        return remote(x_out.at[m], x_in.at[m], dx_s.at[m], dx_r.at[m], (across, lane))

    def end_copy(m, whose):
        return remote(end_out.at[m], end_in.at[whose, 0], e_s.at[m], e_r.at[m], (seg, at(m)))

    def to_core(n, m, whose):
        core_out[n, m] = partial(whose, m).astype(jnp.bfloat16)
        dc_copy(n, m).start()

    def to_chip(m):
        dc_copy(1, m).wait_recv()
        x_out[m] = (partial(across, m) + core_in[1, m].astype(jnp.float32)).astype(jnp.bfloat16)
        dx_copy(m).start()
        to_core(0, m, other)

    def total(m):
        mine = partial(seg, m)
        dc_copy(0, m).wait_recv()
        dx_copy(m).wait_recv()
        near = core_in[0, m].astype(jnp.float32)
        return (mine + near + x_in[m].astype(jnp.float32)).astype(jnp.bfloat16)

    def to_owner(m):
        end_out[m] = total(m)
        end_copy(m, lane).start()

    each(far_first, lambda m: to_core(1, m, beyond))
    each(far_first, to_chip)
    each(far_first[:-1], to_owner)
    od_in[lane] = od[chunk(lane), :]
    each(far_first[:-1], lambda m: od_copy(m, at(m)).wait_recv())
    unpack_pair(od_in, dq_ref, out_ref)
    end_in[lane, 0] = total(0)
    def finish(m):
        for n in range(2):
            c_copy(n, m, seg).wait_send()
            dc_copy(n, m).wait_send()
        x_copy(m, seg).wait_send()
        dx_copy(m).wait_send()

    def finish_lanes(m):
        for copy in (kv_copy, qd_copy, od_copy, end_copy):
            copy(m, lane).wait_send()

    each(far_first, finish)
    each(far_first[:-1], finish_lanes)
    each(near_first, lambda m: end_copy(m, at(m)).wait_recv())


def unpack_pair(block, left, right):
    for h in range(0, block.shape[0], 2):
        columns = slice(h * HDIM, (h + 2) * HDIM)
        left[:, columns] = join(block[h][:, :HDIM], block[h + 1][:, :HDIM])
        right[:, columns] = join(block[h][:, HDIM:], block[h + 1][:, HDIM:])


def write_kernel(out_ref, dq_ref, end_in, out_hbm, dq_hbm, dk_hbm, dv_hbm, dk_ref, dv_ref, sems):
    early = [
        pltpu.make_async_copy(out_ref, out_hbm, sems.at[0]),
        pltpu.make_async_copy(dq_ref, dq_hbm, sems.at[1]),
    ]
    for copy in early:
        copy.start()
    unpack_pair(end_in.at[:, 0], dk_ref, dv_ref)
    late = [
        pltpu.make_async_copy(dk_ref, dk_hbm, sems.at[2]),
        pltpu.make_async_copy(dv_ref, dv_hbm, sems.at[3]),
    ]
    for copy in late:
        copy.start()
    for copy in early + late:
        copy.wait()


def fits(lanes, heads_here, rows):
    return heads_here == 1 and rows == 2 * BLK and 2 * lanes * KSEL == LANES


def fused(lanes, query_rows, key_rows, value_rows, out_grad, block_lists, block_counts):
    rows, width = query_rows.shape
    segs, half, f32 = 4, jnp.bfloat16, jnp.float32
    vmem = pl.BlockSpec(memory_space=pltpu.VMEM)
    hbm = pl.BlockSpec(memory_space=pltpu.HBM)
    dma = pltpu.SemaphoreType.DMA
    lists = block_lists.T
    chunks = (lanes, rows, PAIR)
    buffers = (
        [((rows, width), half)] * 4
        + [(chunks, half), ((lanes, 2, BLK, PAIR), half)]
        + [((lanes * rows, PAIR), half), ((2 * segs * lanes, BLK, PAIR), half), ((lanes * rows, PAIR), half)]
        + [(chunks, half)]
        + [((LANES + 1, BLK, PAIR), f32)]
        + [((2, 2, 2 * BLK, KSEL * BLK), f32), ((2, 2, 2 * BLK, KSEL * BLK), half)]
        + [((2, *chunks), half)] * 2
        + [(chunks, half)] * 3
    )
    size = sum(math.prod(shape) * jnp.dtype(kind).itemsize for shape, kind in buffers)
    return pl.pallas_call(
        functools.partial(fused_kernel, lanes),
        out_shape=[jax.ShapeDtypeStruct((rows, width), half)] * 2
        + [jax.ShapeDtypeStruct((lanes, 1, rows, PAIR), half)],
        in_specs=[hbm] * 6,
        out_specs=[vmem] * 3,
        scratch_shapes=[pltpu.VMEM(*buffer) for buffer in buffers]
        + [pltpu.SMEM(lists.shape, jnp.int32), pltpu.SMEM(block_counts.shape, jnp.int32)]
        + [pltpu.VMEM(lists.shape, jnp.int32), pltpu.VMEM((8, LANES), jnp.int32), pltpu.SMEM((8, LANES), jnp.int32)]
        + [dma((7,)), dma((1,))]
        + [dma((lanes,))] * 6
        + [dma((2, lanes))] * 2
        + [dma((lanes,))] * 6
        + [dma((2, lanes))] * 2,
        compiler_params=pltpu.CompilerParams(
            collective_id=0, has_side_effects=True, vmem_limit_bytes=6 * MIB + size + 8 * lanes * rows * PAIR
        ),
        name="fused",
    )(
        *(
            pltpu.with_memory_space_constraint(a, pltpu.HBM)
            for a in (query_rows, key_rows, value_rows, out_grad, lists, block_counts)
        )
    )


def unpack_kernel(od, dkv, out_ref, dq_ref, dk_ref, dv_ref):
    for block, left, right in ((od, dq_ref, out_ref), (dkv, dk_ref, dv_ref)):
        heads_here = block.shape[1]
        for h in range(0, block.shape[0] * heads_here, 2):
            a, b = (block[g // heads_here, g % heads_here] for g in (h, h + 1))
            columns = slice(h * HDIM, (h + 2) * HDIM)
            left[:, columns] = join(a[:, :HDIM], b[:, :HDIM])
            right[:, columns] = join(a[:, HDIM:], b[:, HDIM:])


def comm_params(number, chunks, block):
    chunk_bytes = 2 * math.prod(block)
    return pltpu.CompilerParams(
        collective_id=number, has_side_effects=True, vmem_limit_bytes=4 * MIB + chunks * chunk_bytes
    )


def staged(lanes, query_rows, key_rows, value_rows, out_grad, block_lists, block_counts):
    rows, width = query_rows.shape
    heads_here = width // HDIM // lanes
    segs = 4
    block = (heads_here, rows, PAIR)
    vmem = pl.BlockSpec(memory_space=pltpu.VMEM)
    dma = pltpu.SemaphoreType.DMA
    half = jnp.bfloat16
    chunks = jax.ShapeDtypeStruct((lanes, *block), half)

    qd, kv = pl.pallas_call(
        functools.partial(gather_kernel, lanes),
        out_shape=(chunks, jax.ShapeDtypeStruct((segs, lanes, *block), half)),
        in_specs=[pl.BlockSpec(memory_space=pltpu.HBM)] * 4,
        out_specs=(vmem, vmem),
        scratch_shapes=[pltpu.VMEM((rows, width), half)] * 4
        + [pltpu.VMEM((lanes, *block), half)] * 2
        + [dma((4,))]
        + [dma((lanes,))] * 6
        + [dma((2, lanes))] * 2,
        compiler_params=comm_params(0, 10 * lanes, block),
        name="gather",
    )(*(pltpu.with_memory_space_constraint(a, pltpu.HBM) for a in (query_rows, key_rows, value_rows, out_grad)))

    qd = qd.transpose(1, 0, 2, 3).reshape(heads_here, lanes * rows, PAIR)
    kv = kv.transpose(2, 0, 1, 3, 4).reshape(heads_here, segs * lanes * rows, PAIR)
    od, dkv = attention(block_lists, block_counts, qd, kv)
    od = od.reshape(heads_here, lanes, rows, PAIR).transpose(1, 0, 2, 3)
    dkv = dkv.reshape(heads_here, segs, lanes, rows, PAIR).transpose(1, 2, 0, 3, 4)

    od, dkv = pl.pallas_call(
        functools.partial(return_kernel, lanes),
        out_shape=[chunks] * 2,
        in_specs=[vmem] * 2,
        out_specs=[vmem] * 2,
        scratch_shapes=[pltpu.VMEM((2, lanes, *block), half)]
        + [pltpu.VMEM((lanes, *block), half)] * 3
        + [dma((lanes + 1,))] * 2
        + [dma((2, lanes + 1))] * 2
        + [dma((lanes + 1,))] * 4,
        compiler_params=comm_params(1, 14 * lanes, block),
        name="scatter",
    )(od, dkv)

    return pl.pallas_call(
        unpack_kernel,
        out_shape=[jax.ShapeDtypeStruct((rows, width), half)] * 4,
        in_specs=[vmem] * 2,
        out_specs=[vmem] * 4,
        compiler_params=pltpu.CompilerParams(vmem_limit_bytes=4 * MIB + 32 * rows * width),
        name="unpack",
    )(od, dkv)


def on_device(lanes, *arrays):
    rows, width = arrays[0].shape
    if not fits(lanes, width // HDIM // lanes, rows):
        return staged(lanes, *arrays)
    half = jnp.bfloat16
    vmem = pl.BlockSpec(memory_space=pltpu.VMEM)
    hbm = pl.BlockSpec(memory_space=pltpu.HBM)
    return pl.pallas_call(
        write_kernel,
        out_shape=[jax.ShapeDtypeStruct((rows, width), half)] * 4,
        in_specs=[vmem] * 3,
        out_specs=[hbm] * 4,
        scratch_shapes=[pltpu.VMEM((rows, width), half)] * 2 + [pltpu.SemaphoreType.DMA((4,))],
        compiler_params=pltpu.CompilerParams(vmem_limit_bytes=4 * MIB + 32 * rows * width),
        name="write",
    )(*fused(lanes, *arrays))


def solution(mesh):
    tokens = P(("blk", "uly"), None)
    return jax.shard_map(
        functools.partial(on_device, mesh.shape["uly"]),
        mesh=mesh,
        in_specs=(tokens, tokens, tokens, tokens, P("blk", None), P("blk")),
        out_specs=(tokens, tokens, tokens, tokens),
        check_vma=False,
    )
```

```python
import functools
import math

import jax
import jax.numpy as jnp
from jax import lax
from jax.experimental import pallas as pl
from jax.experimental.pallas import tpu as pltpu
from jax.sharding import PartitionSpec as P

HDIM = 64
BLK = 64
KSEL = 8
PAIR = 2 * HDIM
SCALE = 1.0 / math.sqrt(HDIM)
GROUP = 16
MIB = 1024 * 1024
LANES = 128


def dot(a, b, dims):
    return lax.dot_general(a, b, (dims, ((), ())), preferred_element_type=jnp.float32)


def attention_kernel(group, lists_hbm, counts_hbm, qd, kv, od, dkv, lists, counts, acc, sems):
    loads = (
        pltpu.make_async_copy(lists_hbm, lists, sems.at[0]),
        pltpu.make_async_copy(counts_hbm, counts, sems.at[1]),
    )
    for load in loads:
        load.start()
    for h in range(qd.shape[0]):
        acc[...] = jnp.zeros_like(acc)
        if h == 0:
            for load in loads:
                load.wait()
        attend_head(group, lists, counts, qd.at[h], kv.at[h], od.at[h], acc)
        dkv[h] = acc[...].astype(dkv.dtype)


def attend_head(group, lists, counts, qd_ref, kv_ref, od_ref, acc):
    local_blocks = qd_ref.shape[0] // BLK
    lane = lax.broadcasted_iota(jnp.int32, (BLK, PAIR), 1)
    first = lane < HDIM
    column = lax.broadcasted_iota(jnp.int32, (BLK, KSEL * BLK), 1)

    def one_block(b):
        rows = pl.ds(pl.multiple_of(b * BLK, BLK), BLK)
        picks = [pl.ds(pl.multiple_of(lists[j, b] * BLK, BLK), BLK) for j in range(KSEL)]
        qd = qd_ref[rows, :]
        zero = jnp.zeros_like(qd)
        diag = jnp.concatenate([jnp.where(first, qd * SCALE, zero), jnp.where(first, zero, qd)], axis=0)
        kv = jnp.concatenate([kv_ref[pick, :] for pick in picks], axis=0)
        both = dot(diag, kv, ((1,), (1,)))
        scores = jnp.where(column < counts[b] * BLK, both[:BLK], -1e30)
        weights = jnp.exp(scores - jnp.max(scores, axis=1, keepdims=True))
        prob = weights * (1.0 / jnp.sum(weights, axis=1, keepdims=True))
        rounded = prob.astype(jnp.bfloat16)
        delta = jnp.sum(rounded.astype(jnp.float32) * both[BLK:], axis=1, keepdims=True)
        grad_score = (prob * (both[BLK:] - delta)).astype(jnp.bfloat16)
        stacked = jnp.concatenate([grad_score, rounded], axis=0)
        rows_out = dot(stacked, kv, ((1,), (0,)))
        od_ref[rows, :] = jnp.where(first, rows_out[:BLK] * SCALE, rows_out[BLK:]).astype(jnp.bfloat16)
        terms = dot(stacked, diag, ((0,), (0,)))
        return picks, terms

    def turn(g, carry):
        done = [one_block(g * group + i) for i in range(group)]
        for picks, terms in done:
            for j, pick in enumerate(picks):
                acc[pick, :] += terms[j * BLK : (j + 1) * BLK]
        return carry

    lax.fori_loop(0, local_blocks // group, turn, 0)

def attention(block_lists, block_counts, qd, kv):
    heads_here, seg_rows, _ = qd.shape
    all_rows = kv.shape[1]
    vmem = pl.BlockSpec(memory_space=pltpu.VMEM)
    hbm = pl.BlockSpec(memory_space=pltpu.HBM)
    lists = block_lists.T
    limit = 6 * MIB + 4 * all_rows * PAIR + 4 * heads_here * (all_rows + seg_rows) * PAIR
    return pl.pallas_call(
        functools.partial(attention_kernel, math.gcd(GROUP, seg_rows // BLK)),
        out_shape=(
            jax.ShapeDtypeStruct(qd.shape, jnp.bfloat16),
            jax.ShapeDtypeStruct(kv.shape, jnp.bfloat16),
        ),
        in_specs=[hbm, hbm, vmem, vmem],
        out_specs=(vmem, vmem),
        scratch_shapes=[
            pltpu.SMEM(lists.shape, jnp.int32),
            pltpu.SMEM(block_counts.shape, jnp.int32),
            pltpu.VMEM((all_rows, PAIR), jnp.float32),
            pltpu.SemaphoreType.DMA((2,)),
        ],
        compiler_params=pltpu.CompilerParams(vmem_limit_bytes=limit),
        name="attention",
    )(
        pltpu.with_memory_space_constraint(lists, pltpu.HBM),
        pltpu.with_memory_space_constraint(block_counts, pltpu.HBM),
        qd,
        kv,
    )


MESH = pl.DeviceIdType.MESH


def places():
    seg, lane = lax.axis_index("blk"), lax.axis_index("uly")
    core = lax.rem(seg, 2)
    return seg, lane, seg + 1 - 2 * core, lax.rem(seg + 2, 4)


def remote(src, dst, send, recv, device):
    return pltpu.make_async_remote_copy(
        src_ref=src, dst_ref=dst, send_sem=send, recv_sem=recv, device_id=device, device_id_type=MESH
    )


def greet(lanes, diagonal=False):
    seg, lane, other, across = places()
    barrier = pltpu.get_barrier_semaphore()

    def one(i, carry):
        device = (seg, lax.rem(lane + i, lanes))
        pl.semaphore_signal(barrier, inc=1, device_id=device, device_id_type=MESH)
        return carry

    lax.fori_loop(1, lanes, one, 0)
    for near in (other, across, lax.rem(other + 2, 4))[: 3 if diagonal else 2]:
        pl.semaphore_signal(barrier, inc=1, device_id=(near, lane), device_id_type=MESH)
    return barrier


def loop(start, stop, body):
    lax.fori_loop(start, stop, lambda i, carry: (body(i), carry)[1], 0)


def join(left, right):
    return jnp.concatenate([left, right], axis=1)


def gather_kernel(
    lanes, q_hbm, k_hbm, v_hbm, g_hbm, qd, kv,
    k_ref, v_ref, q_ref, g_ref, qd_out, kv_out, in_s, qd_s, qd_r, kv_s, kv_r, x_s, x_r, c_s, c_r,
):
    pairs = ((k_hbm, k_ref), (v_hbm, v_ref), (q_hbm, q_ref), (g_hbm, g_ref))
    loads = [pltpu.make_async_copy(*pair, in_s.at[n]) for n, pair in enumerate(pairs)]
    for load in loads:
        load.start()
    seg, lane, other, across = places()
    heads_here = qd.shape[1]
    barrier = greet(lanes, True)

    def pack(left, right, to):
        for h in range(lanes * heads_here):
            columns = slice(h * HDIM, (h + 1) * HDIM)
            to[h // heads_here, h % heads_here] = join(left[:, columns], right[:, columns])

    loads[0].wait()
    loads[1].wait()
    pack(k_ref, v_ref, kv_out)
    pl.semaphore_wait(barrier, lanes + 2)

    def kv_copy(i, target, source):
        return remote(kv_out.at[target], kv.at[seg, source], kv_s.at[i], kv_r.at[i], (seg, target))

    def qd_copy(i, target, source):
        return remote(qd_out.at[target], qd.at[source], qd_s.at[i], qd_r.at[i], (seg, target))

    def x_copy(i, source, whose):
        return remote(kv.at[whose, source], kv.at[whose, source], x_s.at[i], x_r.at[i], (across, lane))

    def c_copy(n, i, source, whose):
        block = kv.at[whose, source]
        near = other if n == 0 else lax.rem(other + 2, 4)
        return remote(block, block, c_s.at[n, i], c_r.at[n, i], (near, lane))

    def ahead(i):
        return lax.rem(lane + i, lanes)

    def behind(i):
        return lax.rem(lane + lanes - i, lanes)

    loop(1, lanes, lambda i: kv_copy(i, ahead(i), lane).start())
    kv[seg, lane] = kv_out[lane]
    x_copy(0, lane, seg).start()
    c_copy(1, 0, lane, seg).start()
    c_copy(0, 0, lane, seg).start()
    loads[2].wait()
    loads[3].wait()
    pack(q_ref, g_ref, qd_out)
    qd[lane] = qd_out[lane]

    def arrive(i):
        kv_copy(i, lane, behind(i)).wait_recv()
        x_copy(i, behind(i), seg).start()
        qd_copy(i, ahead(i), lane).start()
        c_copy(1, i, behind(i), seg).start()
        c_copy(0, i, behind(i), seg).start()

    loop(1, lanes, arrive)
    loop(0, lanes, lambda i: x_copy(i, behind(i), across).wait_recv())

    def finish(i):
        c_copy(0, i, behind(i), other).wait_recv()
        c_copy(1, i, behind(i), lax.rem(other + 2, 4)).wait_recv()
        x_copy(i, behind(i), seg).wait_send()
        c_copy(0, i, behind(i), seg).wait_send()
        c_copy(1, i, behind(i), seg).wait_send()

    loop(0, lanes, finish)

    def finish_lanes(i):
        qd_copy(i, lane, behind(i)).wait_recv()
        qd_copy(i, ahead(i), lane).wait_send()
        kv_copy(i, ahead(i), lane).wait_send()

    loop(1, lanes, finish_lanes)


def return_kernel(
    lanes, od, dkv, od_in, end_in, core_in, x_out, x_in, end_out,
    od_s, od_r, c_s, c_r, x_s, x_r, e_s, e_r,
):
    seg, lane, other, across = places()
    heads_here = od.shape[1]
    barrier = greet(lanes)

    def ahead(i):
        return lax.rem(lane + i, lanes)

    def behind(i):
        return lax.rem(lane + lanes - i, lanes)

    def od_copy(i, target, source):
        return remote(od.at[target], od_in.at[source], od_s.at[i], od_r.at[i], (seg, target))

    def end_copy(i, target, source):
        return remote(end_out.at[target], end_in.at[source], e_s.at[i], e_r.at[i], (seg, target))

    def c_copy(n, i, whose):
        return remote(dkv.at[whose, ahead(i)], core_in.at[n, ahead(i)], c_s.at[n, i], c_r.at[n, i], (other, lane))

    def x_copy(i):
        return remote(x_out.at[ahead(i)], x_in.at[ahead(i)], x_s.at[i], x_r.at[i], (across, lane))

    def send(i):
        c_copy(1, i, lax.rem(other + 2, 4)).start()
        c_copy(0, i, other).start()

    def wide(block):
        return block.astype(jnp.float32)

    def reduce_core(i):
        c_copy(1, i, other).wait_recv()
        to = ahead(i)
        x_out[to] = (wide(dkv[across, to]) + wide(core_in[1, to])).astype(jnp.bfloat16)
        x_copy(i).start()

    def total(i):
        c_copy(0, i, other).wait_recv()
        x_copy(i).wait_recv()
        to = ahead(i)
        return (wide(dkv[seg, to]) + wide(core_in[0, to]) + wide(x_in[to])).astype(jnp.bfloat16)

    def reduce_chip(i):
        end_out[ahead(i)] = total(i)
        end_copy(i, ahead(i), lane).start()

    lag = min(4, lanes - 1)
    pl.semaphore_wait(barrier, lanes + 1)
    loop(1, lanes + 1, send)
    loop(1, lanes, lambda i: od_copy(i, ahead(i), lane).start())
    od_in[lane] = od[lane]
    loop(1, lag + 1, reduce_core)

    def both(i):
        reduce_core(i)
        reduce_chip(i - lag)

    loop(lag + 1, lanes + 1, both)
    loop(lanes + 1 - lag, lanes, reduce_chip)
    end_in[lane] = total(lanes)

    def finish(i):
        c_copy(0, i, other).wait_send()
        c_copy(1, i, other).wait_send()
        x_copy(i).wait_send()

    loop(1, lanes + 1, finish)

    def finish_lanes(i):
        od_copy(i, lane, behind(i)).wait_recv()
        end_copy(i, lane, behind(i)).wait_recv()
        od_copy(i, ahead(i), lane).wait_send()
        end_copy(i, ahead(i), lane).wait_send()

    loop(1, lanes, finish_lanes)


def exchange(lanes, lane, m):
    partner, bit = 0, 1
    while bit < lanes:
        partner += bit * lax.rem(lax.div(lane, bit) + m // bit, 2)
        bit *= 2
    return partner


def chunk_at(lanes, n):
    return lax.rem(n, 2) * (lanes - 1 - n // 2) + lax.rem(n + 1, 2) * (n // 2)


def block_diagonal(qd):
    first = lax.broadcasted_iota(jnp.int32, qd.shape, 1) < HDIM
    zero = jnp.zeros_like(qd)
    return jnp.concatenate([jnp.where(first, qd * SCALE, zero), jnp.where(first, zero, qd)], axis=0)


def block_rows(b):
    return pl.ds(pl.multiple_of(b * BLK, BLK), BLK)


def seen_rows(kv, lists, b):
    return jnp.concatenate([kv[lists[j, b]] for j in range(KSEL)], axis=0)


def score_block(qd, kv, lists, b, both):
    both[...] = dot(block_diagonal(qd[block_rows(b), :]), seen_rows(kv, lists, b), ((1,), (1,)))


def softmax_block(counts, b, both, stacked):
    column = lax.broadcasted_iota(jnp.int32, (1, KSEL * BLK), 1)
    scores = jnp.where(column < counts[b] * BLK, both[:BLK, :], -1e30)
    weights = jnp.exp(scores - jnp.max(scores, axis=1, keepdims=True))
    prob = weights * (1.0 / jnp.sum(weights, axis=1, keepdims=True))
    stacked[BLK:, :] = prob.astype(jnp.bfloat16)
    grad_prob = both[BLK:, :]
    delta = jnp.sum(prob * grad_prob, axis=1, keepdims=True)
    stacked[:BLK, :] = (prob * (grad_prob - delta)).astype(jnp.bfloat16)


def gradient_block(qd, kv, lists, chain, b, slot, stacked, od, sums):
    first = lax.broadcasted_iota(jnp.int32, (BLK, PAIR), 1) < HDIM
    both = stacked[...]
    rows_out = dot(both, seen_rows(kv, lists, b), ((1,), (0,)))
    od[block_rows(b), :] = jnp.where(first, rows_out[:BLK] * SCALE, rows_out[BLK:]).astype(jnp.bfloat16)
    terms = dot(both, block_diagonal(qd[block_rows(b), :]), ((0,), (0,)))
    for j in range(KSEL):
        before = sums[chain[0, j * (LANES // KSEL) + b]]
        sums[slot + j] = before + terms[j * BLK : (j + 1) * BLK]


def link_terms(lanes, seg, lane, lists, out):
    blocks = 2 * lanes

    def iota(shape, axis):
        return lax.broadcasted_iota(jnp.int32, shape, axis)

    def parts(axis):
        entry = iota((LANES, LANES), axis)
        j, b = lax.div(entry, blocks), lax.rem(entry, blocks)
        m = jnp.bitwise_xor(lax.div(b, 2), lane)
        turn = jnp.where(m < lanes // 2, 2 * m, 2 * (lanes - 1 - m) + 1)
        return j, b, 2 * turn + lax.rem(b, 2)

    wide = jnp.concatenate([lists[...]] * (LANES // blocks), axis=1)
    own_row = iota((KSEL, LANES), 0) == lax.div(iota((KSEL, LANES), 1), blocks)
    row = jnp.sum(jnp.where(own_row, wide, 0), axis=0, keepdims=True)
    across = jnp.broadcast_to(row, (LANES, LANES))
    down = across.T
    j, b, when = parts(0)
    now = parts(1)[2]
    slot = KSEL * when + j
    valid = jnp.logical_or(j == 0, down != seg * blocks + b)
    earlier = jnp.logical_and(jnp.logical_and(down == across, when < now), valid)
    same = jnp.logical_and(down == iota((LANES, LANES), 1), valid)
    for n, chosen in enumerate((earlier, same)):
        latest = jnp.max(jnp.where(chosen, slot, -1), axis=0, keepdims=True)
        out[n : n + 1, :] = jnp.where(latest < 0, LANES, latest)


def fused_kernel(
    lanes, q_hbm, k_hbm, v_hbm, g_hbm, lists_hbm, counts_hbm, out_ref, dq_ref, end_in,
    k_ref, v_ref, q_ref, g_ref, qd_out, kv_out, qd, kv, od, od_in, sums, both, stacked,
    core_out, core_in, x_out, x_in, end_out, lists, counts, lists_v, chain_v, chain,
    in_s, idx_s, kv_s, kv_r, qd_s, qd_r, x_s, x_r, c_s, c_r, od_s, od_r, e_s, e_r, dx_s, dx_r, dc_s, dc_r,
):
    rows = q_hbm.shape[0]
    half = lanes // 2
    pairs = (
        (k_hbm, k_ref), (v_hbm, v_ref), (q_hbm, q_ref), (g_hbm, g_ref),
        (lists_hbm, lists_v), (lists_hbm, lists), (counts_hbm, counts),
    )
    loads = [pltpu.make_async_copy(*pair, in_s.at[n]) for n, pair in enumerate(pairs)]
    seg, lane, other, across = places()
    beyond = lax.rem(other + 2, 4)
    partners = [exchange(lanes, lane, m) for m in range(lanes)]
    barrier = pltpu.get_barrier_semaphore()
    for device in [(seg, partners[m]) for m in range(lanes - 1, 0, -1)] + [(across, lane), (other, lane)]:
        pl.semaphore_signal(barrier, inc=1, device_id=device, device_id_type=MESH)
    for load in loads:
        load.start()

    def at(m):
        return partners[m] if isinstance(m, int) else exchange(lanes, lane, m)

    def each(order, body):
        for m in order:
            body(m)

    def pack(left, right, to):
        for h in range(lanes):
            columns = slice(h * HDIM, (h + 1) * HDIM)
            to[h] = join(left[:, columns], right[:, columns]).reshape(to.shape[1:])

    def chunk(i):
        return pl.ds(pl.multiple_of(i * rows, rows), rows)

    def piece(whose, i):
        return kv.at[pl.ds(2 * (whose * lanes + i), 2)]

    def kv_copy(m, whose):
        return remote(kv_out.at[at(m)], piece(seg, whose), kv_s.at[m], kv_r.at[m], (seg, at(m)))

    def qd_copy(m, whose):
        return remote(qd_out.at[at(m)], qd.at[chunk(whose), :], qd_s.at[m], qd_r.at[m], (seg, at(m)))

    def x_copy(m, whose):
        block = piece(whose, at(m))
        return remote(block, block, x_s.at[m], x_r.at[m], (across, lane))

    def c_copy(n, m, whose):
        block = piece(whose, at(m))
        return remote(block, block, c_s.at[n, m], c_r.at[n, m], (other, lane))

    def od_copy(m, whose):
        return remote(od.at[chunk(at(m)), :], od_in.at[whose], od_s.at[m], od_r.at[m], (seg, at(m)))

    def send_kv(m):
        kv_copy(m, lane).start()

    def send_qd(m):
        qd_copy(m, lane).start()

    def forward(m):
        x_copy(m, across).wait_recv()
        c_copy(1, m, across).start()

    def to_near(m):
        x_copy(m, seg).start()
        c_copy(0, m, seg).start()

    def arrive(m):
        kv_copy(m, at(m)).wait_recv()
        to_near(m)

    loads[0].wait()
    loads[1].wait()
    pack(k_ref, v_ref, kv_out)
    pl.semaphore_wait(barrier, lanes + 1)
    for k in range(1, half):
        send_kv(lanes - k)
        send_kv(k)
    send_kv(half)
    kv[pl.ds(2 * (seg * lanes + lane), 2)] = kv_out[lane]
    to_near(0)
    loads[2].wait()
    loads[3].wait()
    pack(q_ref, g_ref, qd_out)
    qd[chunk(lane), :] = qd_out[lane]
    loads[4].wait()
    link_terms(lanes, seg, lane, lists_v, chain_v)
    chain_copy = pltpu.make_async_copy(chain_v, chain, idx_s.at[0])
    chain_copy.start()
    sums[LANES] = jnp.zeros((BLK, PAIR), jnp.float32)

    near_first = list(range(1, half)) + list(range(lanes - 1, half - 1, -1))
    far_first = list(range(lanes - 1, -1, -1))
    each(near_first, arrive)
    for m in far_first[:half]:
        send_qd(m)
        if m > half:
            send_qd(lanes - m)
    each([0] + near_first, forward)

    def complete(m):
        c_copy(0, m, other).wait_recv()
        c_copy(1, m, beyond).wait_recv()

    each(far_first, complete)
    loads[5].wait()
    loads[6].wait()
    chain_copy.wait()

    def score(n, slot):
        for i in range(2):
            score_block(qd, kv, lists, 2 * at(chunk_at(lanes, n)) + i, both.at[slot, i])

    def softmax(n, slot):
        for i in range(2):
            softmax_block(counts, 2 * at(chunk_at(lanes, n)) + i, both.at[slot, i], stacked.at[slot, i])

    def gradient(n, slot):
        for i in range(2):
            block = 2 * at(chunk_at(lanes, n)) + i
            gradient_block(qd, kv, lists, chain, block, (2 * n + i) * KSEL, stacked.at[slot, i], od, sums)

    def receive_qd(n):
        m = chunk_at(lanes, n)
        qd_copy(m, at(m)).wait_recv()

    def send_od(n):
        od_copy(chunk_at(lanes, n), lane).start()

    score(0, 0)
    receive_qd(1)
    softmax(0, 0)
    score(1, 1)

    def two_steps(n):
        receive_qd(n)
        gradient(n - 2, 0)
        softmax(n - 1, 1)
        score(n, 0)

        @pl.when(n > 2)
        def _():
            send_od(n - 2)

        receive_qd(n + 1)
        gradient(n - 1, 1)
        softmax(n, 0)
        score(n + 1, 1)
        send_od(n - 1)

    loop(1, half, lambda k: two_steps(2 * k))
    gradient(lanes - 2, 0)
    softmax(lanes - 1, 1)
    send_od(lanes - 2)
    gradient(lanes - 1, 1)
    send_od(lanes - 1)

    def partial(whose, m):
        block = 2 * (whose * lanes + at(m))
        return jnp.concatenate([sums[chain[1, block + i]] for i in range(2)], axis=0)

    def dc_copy(n, m):
        return remote(core_out.at[n, m], core_in.at[n, m], dc_s.at[n, m], dc_r.at[n, m], (other, lane))

    def dx_copy(m):
        return remote(x_out.at[m], x_in.at[m], dx_s.at[m], dx_r.at[m], (across, lane))

    def end_copy(m, whose):
        return remote(end_out.at[m], end_in.at[whose, 0], e_s.at[m], e_r.at[m], (seg, at(m)))

    def to_core(n, m, whose):
        core_out[n, m] = partial(whose, m).astype(jnp.bfloat16)
        dc_copy(n, m).start()

    def to_chip(m):
        dc_copy(1, m).wait_recv()
        x_out[m] = (partial(across, m) + core_in[1, m].astype(jnp.float32)).astype(jnp.bfloat16)
        dx_copy(m).start()
        to_core(0, m, other)

    def total(m):
        mine = partial(seg, m)
        dc_copy(0, m).wait_recv()
        dx_copy(m).wait_recv()
        near = core_in[0, m].astype(jnp.float32)
        return (mine + near + x_in[m].astype(jnp.float32)).astype(jnp.bfloat16)

    def to_owner(m):
        end_out[m] = total(m)
        end_copy(m, lane).start()

    back = [m for k in range(1, half + 1) for m in (lanes - k, half - k)]
    each(back, lambda m: to_core(1, m, beyond))
    each(back, to_chip)
    each(back[:-1], to_owner)
    od_in[lane] = od[chunk(lane), :]
    each(far_first[:-1], lambda m: od_copy(m, at(m)).wait_recv())
    unpack_pair(od_in, dq_ref, out_ref)
    end_in[lane, 0] = total(0)
    def finish(m):
        for n in range(2):
            c_copy(n, m, seg).wait_send()
            dc_copy(n, m).wait_send()
        x_copy(m, seg).wait_send()
        dx_copy(m).wait_send()

    def finish_lanes(m):
        for copy in (kv_copy, qd_copy, od_copy, end_copy):
            copy(m, lane).wait_send()

    each(far_first, finish)
    each(far_first[:-1], finish_lanes)
    each(near_first, lambda m: end_copy(m, at(m)).wait_recv())


def unpack_pair(block, left, right):
    for h in range(0, block.shape[0], 2):
        columns = slice(h * HDIM, (h + 2) * HDIM)
        left[:, columns] = join(block[h][:, :HDIM], block[h + 1][:, :HDIM])
        right[:, columns] = join(block[h][:, HDIM:], block[h + 1][:, HDIM:])


def write_kernel(out_ref, dq_ref, end_in, out_hbm, dq_hbm, dk_hbm, dv_hbm, dk_ref, dv_ref, sems):
    early = [
        pltpu.make_async_copy(out_ref, out_hbm, sems.at[0]),
        pltpu.make_async_copy(dq_ref, dq_hbm, sems.at[1]),
    ]
    for copy in early:
        copy.start()
    unpack_pair(end_in.at[:, 0], dk_ref, dv_ref)
    late = [
        pltpu.make_async_copy(dk_ref, dk_hbm, sems.at[2]),
        pltpu.make_async_copy(dv_ref, dv_hbm, sems.at[3]),
    ]
    for copy in late:
        copy.start()
    for copy in early + late:
        copy.wait()


def fits(lanes, heads_here, rows):
    return heads_here == 1 and rows == 2 * BLK and 2 * lanes * KSEL == LANES


def fused(lanes, query_rows, key_rows, value_rows, out_grad, block_lists, block_counts):
    rows, width = query_rows.shape
    segs, half, f32 = 4, jnp.bfloat16, jnp.float32
    vmem = pl.BlockSpec(memory_space=pltpu.VMEM)
    hbm = pl.BlockSpec(memory_space=pltpu.HBM)
    dma = pltpu.SemaphoreType.DMA
    lists = block_lists.T
    chunks = (lanes, rows, PAIR)
    buffers = (
        [((rows, width), half)] * 4
        + [(chunks, half), ((lanes, 2, BLK, PAIR), half)]
        + [((lanes * rows, PAIR), half), ((2 * segs * lanes, BLK, PAIR), half), ((lanes * rows, PAIR), half)]
        + [(chunks, half)]
        + [((LANES + 1, BLK, PAIR), f32)]
        + [((2, 2, 2 * BLK, KSEL * BLK), f32), ((2, 2, 2 * BLK, KSEL * BLK), half)]
        + [((2, *chunks), half)] * 2
        + [(chunks, half)] * 3
    )
    size = sum(math.prod(shape) * jnp.dtype(kind).itemsize for shape, kind in buffers)
    return pl.pallas_call(
        functools.partial(fused_kernel, lanes),
        out_shape=[jax.ShapeDtypeStruct((rows, width), half)] * 2
        + [jax.ShapeDtypeStruct((lanes, 1, rows, PAIR), half)],
        in_specs=[hbm] * 6,
        out_specs=[vmem] * 3,
        scratch_shapes=[pltpu.VMEM(*buffer) for buffer in buffers]
        + [pltpu.SMEM(lists.shape, jnp.int32), pltpu.SMEM(block_counts.shape, jnp.int32)]
        + [pltpu.VMEM(lists.shape, jnp.int32), pltpu.VMEM((8, LANES), jnp.int32), pltpu.SMEM((8, LANES), jnp.int32)]
        + [dma((7,)), dma((1,))]
        + [dma((lanes,))] * 6
        + [dma((2, lanes))] * 2
        + [dma((lanes,))] * 6
        + [dma((2, lanes))] * 2,
        compiler_params=pltpu.CompilerParams(
            collective_id=0, has_side_effects=True, vmem_limit_bytes=6 * MIB + size + 8 * lanes * rows * PAIR
        ),
        name="fused",
    )(
        *(
            pltpu.with_memory_space_constraint(a, pltpu.HBM)
            for a in (query_rows, key_rows, value_rows, out_grad, lists, block_counts)
        )
    )


def unpack_kernel(od, dkv, out_ref, dq_ref, dk_ref, dv_ref):
    for block, left, right in ((od, dq_ref, out_ref), (dkv, dk_ref, dv_ref)):
        heads_here = block.shape[1]
        for h in range(0, block.shape[0] * heads_here, 2):
            a, b = (block[g // heads_here, g % heads_here] for g in (h, h + 1))
            columns = slice(h * HDIM, (h + 2) * HDIM)
            left[:, columns] = join(a[:, :HDIM], b[:, :HDIM])
            right[:, columns] = join(a[:, HDIM:], b[:, HDIM:])


def comm_params(number, chunks, block):
    chunk_bytes = 2 * math.prod(block)
    return pltpu.CompilerParams(
        collective_id=number, has_side_effects=True, vmem_limit_bytes=4 * MIB + chunks * chunk_bytes
    )


def staged(lanes, query_rows, key_rows, value_rows, out_grad, block_lists, block_counts):
    rows, width = query_rows.shape
    heads_here = width // HDIM // lanes
    segs = 4
    block = (heads_here, rows, PAIR)
    vmem = pl.BlockSpec(memory_space=pltpu.VMEM)
    dma = pltpu.SemaphoreType.DMA
    half = jnp.bfloat16
    chunks = jax.ShapeDtypeStruct((lanes, *block), half)

    qd, kv = pl.pallas_call(
        functools.partial(gather_kernel, lanes),
        out_shape=(chunks, jax.ShapeDtypeStruct((segs, lanes, *block), half)),
        in_specs=[pl.BlockSpec(memory_space=pltpu.HBM)] * 4,
        out_specs=(vmem, vmem),
        scratch_shapes=[pltpu.VMEM((rows, width), half)] * 4
        + [pltpu.VMEM((lanes, *block), half)] * 2
        + [dma((4,))]
        + [dma((lanes,))] * 6
        + [dma((2, lanes))] * 2,
        compiler_params=comm_params(0, 10 * lanes, block),
        name="gather",
    )(*(pltpu.with_memory_space_constraint(a, pltpu.HBM) for a in (query_rows, key_rows, value_rows, out_grad)))

    qd = qd.transpose(1, 0, 2, 3).reshape(heads_here, lanes * rows, PAIR)
    kv = kv.transpose(2, 0, 1, 3, 4).reshape(heads_here, segs * lanes * rows, PAIR)
    od, dkv = attention(block_lists, block_counts, qd, kv)
    od = od.reshape(heads_here, lanes, rows, PAIR).transpose(1, 0, 2, 3)
    dkv = dkv.reshape(heads_here, segs, lanes, rows, PAIR).transpose(1, 2, 0, 3, 4)

    od, dkv = pl.pallas_call(
        functools.partial(return_kernel, lanes),
        out_shape=[chunks] * 2,
        in_specs=[vmem] * 2,
        out_specs=[vmem] * 2,
        scratch_shapes=[pltpu.VMEM((2, lanes, *block), half)]
        + [pltpu.VMEM((lanes, *block), half)] * 3
        + [dma((lanes + 1,))] * 2
        + [dma((2, lanes + 1))] * 2
        + [dma((lanes + 1,))] * 4,
        compiler_params=comm_params(1, 14 * lanes, block),
        name="scatter",
    )(od, dkv)

    return pl.pallas_call(
        unpack_kernel,
        out_shape=[jax.ShapeDtypeStruct((rows, width), half)] * 4,
        in_specs=[vmem] * 2,
        out_specs=[vmem] * 4,
        compiler_params=pltpu.CompilerParams(vmem_limit_bytes=4 * MIB + 32 * rows * width),
        name="unpack",
    )(od, dkv)


def on_device(lanes, *arrays):
    rows, width = arrays[0].shape
    if not fits(lanes, width // HDIM // lanes, rows):
        return staged(lanes, *arrays)
    half = jnp.bfloat16
    vmem = pl.BlockSpec(memory_space=pltpu.VMEM)
    hbm = pl.BlockSpec(memory_space=pltpu.HBM)
    return pl.pallas_call(
        write_kernel,
        out_shape=[jax.ShapeDtypeStruct((rows, width), half)] * 4,
        in_specs=[vmem] * 3,
        out_specs=[hbm] * 4,
        scratch_shapes=[pltpu.VMEM((rows, width), half)] * 2 + [pltpu.SemaphoreType.DMA((4,))],
        compiler_params=pltpu.CompilerParams(vmem_limit_bytes=4 * MIB + 32 * rows * width),
        name="write",
    )(*fused(lanes, *arrays))


def solution(mesh):
    tokens = P(("blk", "uly"), None)
    return jax.shard_map(
        functools.partial(on_device, mesh.shape["uly"]),
        mesh=mesh,
        in_specs=(tokens, tokens, tokens, tokens, P("blk", None), P("blk")),
        out_specs=(tokens, tokens, tokens, tokens),
        check_vma=False,
    )
```
